32 devices in a mesh: row: 4 (over x, core), col: 8 (over z, y).
Axes of the slice: x: 2, y: 2, z: 4, core: 2. Of those that a mesh axis runs over, the one named last changes fastest.
Arguments:
- depth: float32 [3072, 8192], P('row', 'col'), may hold values from 0.05 to 2
- ground: float32 [3072, 8192], P('row', 'col'), may hold values from -4 to 4
- flow_rows: float32 [3072, 8192], P('row', 'col'), may hold values from -3 to 3
- flow_cols: float32 [3072, 8192], P('row', 'col'), may hold values from -3 to 3
- wet_tiles: int32 [4, 8], P('row', 'col'), may hold values 0 or 1
- inlet_cell: int32 [4, 8, 4096], P('row', 'col'), may hold values from 0 to 786431
- inlet_node: int32 [4, 8, 4096], P('row', 'col'), may hold values from 0 to 2047
- inlet_coef: float32 [4, 8, 4096], P('row', 'col'), may hold values from 0.05 to 0.5
- shift_rows: int32 [4, 8], P('row', 'col'), may hold values from 0 to 2, as said below
- shift_cols: int32 [4, 8], P('row', 'col'), may hold values from 0 to 2, as said below
Outputs:
- depth_out: float32 [3072, 8192], P('row', 'col')
- rows_out: float32 [3072, 8192], P('row', 'col')
- cols_out: float32 [3072, 8192], P('row', 'col')
- node_inflow: float32 [2048], P(('row', 'col'))
- moved_rows: float32 [3, 1024, 8192], P(None, 'row', 'col')
- moved_cols: float32 [3, 3072, 2048], P(None, 'row', 'col')
The draws below stay inside these ranges and needn't reach their ends.
Inputs may be any that keep to these rules, and one draw needn't show every extreme that they name: `shift_rows`: some tile reaches 2 in every draw. `shift_cols`: some tile reaches 2 in every draw.
All inputs are finite; a program needn't handle non-finite values. No bound on the sum of `wet_tiles` on one device may be relied on, other than what follows from the above.
Results may differ from the reference program's by a relative error of at most 0.00002.
Values sent between devices are 32-bit elements; how exact they have to be, the bound alone decides.
A program may use at most 128 MiB of HBM per device.

```python
import math
import jax
import jax.numpy as jnp

CX = 768
CY = 1024
STEPS = 3
BLOCK = 128
MAX_BLOCKS = 2
INLET_DEV = 4096
NX = 3072
NY = 8192
NODES = 2048
N_ROW = 4
N_COL = 8


def pick_counts(key):
    total = N_ROW * N_COL
    base = jax.random.randint(key, (total,), 0, MAX_BLOCKS + 1)
    spot = jax.random.randint(jax.random.fold_in(key, 7), (), 0, total)
    return base.at[spot].set(MAX_BLOCKS).reshape(N_ROW, N_COL).astype(jnp.int32)


def draw_shift_rows(key, part):
    return pick_counts(jax.random.fold_in(key, 1))


def draw_shift_cols(key, part):
    return pick_counts(jax.random.fold_in(key, 2))


def plant(result, stream_key, least, largest):
    longest = result.shape.index(max(result.shape))
    spots = []
    for shift in (0, 1):
        where = [jax.random.randint(jax.random.fold_in(stream_key, axis), (), 0, length) for axis, length in enumerate(result.shape)]
        where[longest] = (where[longest] + shift) % result.shape[longest]
        spots.append(tuple(where))
    return result.at[spots[0]].set(least).at[spots[1]].set(largest)


def level_of(stream_key, extent, cuts, low, top_value):
    def one(position, parts):
        draws = jax.random.uniform(jax.random.fold_in(jax.random.fold_in(stream_key, 6), position), (parts,), jnp.float32, low / len(cuts), top_value / len(cuts))
        return jnp.repeat(jnp.exp(draws), extent[position] // parts).reshape((-1,) + (1,) * (len(extent) - position - 1))

    gain = one(*cuts[0])
    for cut in cuts[1:]:
        gain = gain * one(*cut)
    return gain


def normal_values(key, dims, width, most, shards=(), kind=jnp.bfloat16):
    result = width * jax.random.normal(key, dims, jnp.float32)
    if shards:
        result = result * level_of(key, dims, shards, -0.22, 0.18)
    return jnp.clip(result, -most, most).astype(kind)


def setup_inputs(seed: int = 0) -> dict:
    keys = jax.random.split(jax.random.key(seed), 11)
    depth = jnp.clip(jnp.exp(math.log(2.0) - 3.6888794 * jax.random.uniform(keys[0], (NX, NY), jnp.float32) ** level_of(keys[0], (NX, NY), ((0, 4), (1, 8)), -0.2, 0.2)), 0.05, 2.0)
    ground = normal_values(keys[1], (NX, NY), 0.3, 4.0, ((0, 4), (1, 8)), jnp.float32)
    flow_rows = normal_values(keys[2], (NX, NY), 0.2, 3.0, ((0, 4), (1, 8)), jnp.float32)
    flow_cols = normal_values(keys[3], (NX, NY), 0.2, 3.0, ((0, 4), (1, 8)), jnp.float32)
    wet_tiles = plant((jax.random.randint(keys[4], (N_ROW, N_COL), 0, 4) < 3).astype(jnp.int32), jax.random.fold_in(keys[4], 1), 0, 1)
    inlet_cell = plant(jax.random.randint(keys[5], (N_ROW, N_COL, INLET_DEV), 0, CX * CY), jax.random.fold_in(keys[5], 1), 0, (CX * CY) - 1).astype(jnp.int32)
    inlet_node = plant(jax.random.randint(keys[6], (N_ROW, N_COL, INLET_DEV), 0, NODES), jax.random.fold_in(keys[6], 1), 0, NODES - 1).astype(jnp.int32)
    inlet_coef = jnp.clip(jnp.exp(math.log(0.5) - 2.3025851 * jax.random.uniform(keys[7], (N_ROW, N_COL, INLET_DEV), jnp.float32) ** level_of(keys[7], (N_ROW, N_COL, INLET_DEV), ((0, 4), (1, 8)), -0.2, 0.2)), 0.05, 0.5)
    shift_rows = draw_shift_rows(jax.random.fold_in(keys[10], 71), 0)
    shift_cols = draw_shift_cols(jax.random.fold_in(keys[10], 71), 0)
    return dict(depth=depth, ground=ground, flow_rows=flow_rows, flow_cols=flow_cols, wet_tiles=wet_tiles, inlet_cell=inlet_cell, inlet_node=inlet_node, inlet_coef=inlet_coef, shift_rows=shift_rows, shift_cols=shift_cols)


gravity = 9.81
time_step = 0.1
friction = 0.0025
depth_floor = 0.25


def face_update(flow, eta, eta_next, ground, ground_next):
    top = jnp.maximum(eta, eta_next) - jnp.maximum(ground, ground_next)
    face_depth = jnp.maximum(top, 0.0)
    floored = jnp.maximum(face_depth, depth_floor)
    pushed = flow - gravity * time_step * face_depth * (eta_next - eta)
    return pushed / (1.0 + gravity * time_step * friction * jnp.abs(flow) / floored ** (7.0 / 3.0))


def reference(depth, ground, flow_rows, flow_cols, wet_tiles, inlet_cell, inlet_node, inlet_coef, shift_rows, shift_cols):
    wet = jnp.repeat(jnp.repeat(wet_tiles > 0, CX, axis=0), CY, axis=1)
    ground_pad = jnp.pad(ground, 1)
    for step in range(STEPS):
        eta_pad = jnp.pad(depth, 1) + ground_pad
        eta = eta_pad[1:-1, 1:-1]
        new_rows = face_update(flow_rows, eta, eta_pad[2:, 1:-1], ground, ground_pad[2:, 1:-1])
        new_cols = face_update(flow_cols, eta, eta_pad[1:-1, 2:], ground, ground_pad[1:-1, 2:])
        new_rows = jnp.where(wet, new_rows, flow_rows)
        new_cols = jnp.where(wet, new_cols, flow_cols)
        rows_pad = jnp.pad(new_rows, 1)
        cols_pad = jnp.pad(new_cols, 1)
        new_depth = depth + time_step * (rows_pad[:-2, 1:-1] - new_rows + cols_pad[1:-1, :-2] - new_cols)
        depth = jnp.where(wet, new_depth, depth)
        flow_rows, flow_cols = new_rows, new_cols
    tile_row = jnp.arange(N_ROW).astype(jnp.int32)[:, None, None]
    tile_col = jnp.arange(N_COL).astype(jnp.int32)[None, :, None]
    global_row = tile_row * CX + inlet_cell // CY
    global_col = tile_col * CY + inlet_cell % CY
    captured = inlet_coef * jnp.maximum(depth[global_row, global_col], 0.0)
    node_inflow = jax.ops.segment_sum(captured.reshape(-1), inlet_node.reshape(-1), num_segments=NODES)
    state = jnp.stack([depth, flow_rows, flow_cols])
    span = MAX_BLOCKS * BLOCK
    offsets = jnp.arange(span).astype(jnp.int32)
    by_rows = state.reshape(3, N_ROW, CX, NY)[:, :, CX - span:, :]
    keep_rows = jnp.repeat(shift_rows, CY, axis=1)
    mask_rows = offsets[None, :, None] >= (MAX_BLOCKS - keep_rows[:, None, :]) * BLOCK
    by_rows = jnp.where(mask_rows[None], by_rows, 0.0)
    by_rows = jnp.concatenate([jnp.zeros_like(by_rows[:, :1]), by_rows[:, :-1]], axis=1)
    moved_rows = by_rows.reshape(3, N_ROW * span, NY)
    by_cols = state.reshape(3, NX, N_COL, CY)[:, :, :, CY - span:]
    keep_cols = jnp.repeat(shift_cols, CX, axis=0)
    mask_cols = offsets[None, None, :] >= (MAX_BLOCKS - keep_cols[:, :, None]) * BLOCK
    by_cols = jnp.where(mask_cols[None], by_cols, 0.0)
    by_cols = jnp.concatenate([jnp.zeros_like(by_cols[:, :, :1]), by_cols[:, :, :-1]], axis=2)
    moved_cols = by_cols.reshape(3, NX, N_COL * span)
    return depth, flow_rows, flow_cols, node_inflow, moved_rows, moved_cols
```

```python
import functools

import jax
import jax.numpy as jnp
from jax import lax
from jax.experimental import pallas as pl
from jax.experimental.pallas import tpu as pltpu
from jax.sharding import PartitionSpec as P

STEPS = 3
BLOCK = 128
MAX_BLOCKS = 2
NODE_DEV = 64
LANES = 128
SUB = 8
EDGE = 4
GROUP = 2
SEG = 128
MESH = pl.DeviceIdType.MESH


gravity = 9.81
time_step = 0.1
friction = 0.0025
depth_floor = 0.25
POWER = -7.0 / 3.0


def face_update(flow, eta, eta_next, top, pull, rub):
    over = jnp.maximum(eta, eta_next) - top
    root = jnp.exp2(POWER * lax.log2(jnp.maximum(over, depth_floor)))
    drag = rub * jnp.abs(flow) * root
    pushed = flow - pull * jnp.maximum(over, 0.0) * (eta_next - eta)
    return pushed * pl.reciprocal(1.0 + drag)


def fused_kernel(counts, *refs):
    depth, ground, frow, fcol, wet, shift_rows, shift_cols, cells, nodes, coefs = refs[:10]
    out_d, out_f, out_c, moved_rows, moved_cols, extra = refs[10:16]
    (d, g, f, c, w, w8, zr, zc, fin, low, high, packed, near, far, got_top, got_bottom, got_left, got_right, side,
     cell_v, node_v, coef_v, spot_v, picked, acc, parts, slots, note,
     flag_s, spot_s,
     in_sem, edge_sem, small_sem, halo_send, halo_recv, out_sem, col_send, col_recv, row_send, row_recv,
     node_send, node_recv) = refs[16:]
    n_row, n_col = counts
    devices = n_row * n_col
    rows, width = depth.shape
    n = width // LANES + 1
    windows = rows // SEG
    win = SEG + 24
    tall = windows * win
    span = MAX_BLOCKS * BLOCK
    me_row, me_col = lax.axis_index("row"), lax.axis_index("col")
    me = me_row * n_col + me_col
    moves = [(-1, 0), (1, 0), (0, -1), (0, 1), (-1, -1), (-1, 1), (1, -1), (1, 1)]
    arrays = ((depth, d), (ground, g), (frow, f), (fcol, c))

    def place(k):
        other = lax.rem(me + k, devices)
        return other, (other // n_col, lax.rem(other, n_col))

    def there(dr, dc):
        r, q = me_row + dr, me_col + dc
        inside = jnp.logical_and(jnp.logical_and(r >= 0, r < n_row), jnp.logical_and(q >= 0, q < n_col))
        return inside, (r, q)

    for ref in (got_top, got_bottom, got_left, got_right):
        ref[...] = jnp.zeros_like(ref)
    barrier = pltpu.get_barrier_semaphore()

    @pl.loop(1, devices)
    def _(k):
        pl.semaphore_signal(barrier, inc=1, device_id=place(k)[1], device_id_type=MESH)

    small = [pltpu.make_async_copy(src, dst, small_sem.at[k]) for k, (src, dst) in enumerate((
        (wet, flag_s.at[0]), (shift_rows, flag_s.at[1]), (shift_cols, flag_s.at[2]),
        (cells, cell_v), (nodes, node_v), (coefs, coef_v)))]
    for copy in small:
        copy.start()
    edges = []
    for a, (src, _) in enumerate(arrays):
        for k, (piece, dst) in enumerate((
            (src.at[:, pl.ds(0, LANES)], low.at[a]),
            (src.at[:, pl.ds(width - LANES, LANES)], high.at[a]),
            (src.at[pl.ds(0, SUB), :], near.at[pl.ds(a * SUB, SUB), :]),
            (src.at[pl.ds(rows - SUB, SUB), :], far.at[pl.ds(a * SUB, SUB), :]),
        )):
            edges.append(pltpu.make_async_copy(piece, dst, edge_sem.at[a, k]))
            edges[-1].start()

    def loads(s, kind):
        lead, trail = (0 if kind == "top" else SUB), (0 if kind == "bottom" else SUB)
        start = (windows - 1 - s) * SEG - lead
        at = s * win + SUB - lead
        if not isinstance(s, int):
            start, at = pl.multiple_of(start, SUB), pl.multiple_of(at, SUB)
        high_rows = SEG + lead + trail
        return [pltpu.make_async_copy(src.at[pl.ds(start, high_rows), pl.ds(i * LANES, LANES)],
                                      dst.at[pl.ds(i * tall + at, high_rows)], in_sem.at[s, a, i])
                for a, (src, dst) in enumerate(arrays) for i in range(n - 1)]

    def all_loads(s, act):
        for kind, holds in (("bottom", s == 0), ("top", s == windows - 1),
                            ("middle", jnp.logical_and(s > 0, s < windows - 1))):
            @pl.when(holds)
            def _():
                for copy in loads(s, kind):
                    act(copy)

    for copy in loads(0, "bottom"):
        copy.start()

    blank = jnp.zeros((SUB, LANES), jnp.float32)
    for buf in (d, g):
        for i in range(n):
            for s in range(windows):
                buf[pl.ds(i * tall + s * win + SEG + 16, SUB), :] = blank
    for copy in small[:3]:
        copy.wait()
    wet_value = flag_s[0, 0, 0].astype(jnp.float32)
    give_rows = flag_s[1, 0, 0].astype(jnp.float32)
    give_cols = flag_s[2, 0, 0].astype(jnp.float32)
    for ref in (near, far):
        ref[pl.ds(4 * SUB, SUB), :] = jnp.full((SUB, width), wet_value)
        ref[pl.ds(5 * SUB, SUB), :] = jnp.full((SUB, width), give_rows)
    for copy in edges:
        copy.wait()
    lane = lax.broadcasted_iota(jnp.int32, (LANES, LANES), 1)
    own = jnp.where(lane < 5 * SUB, wet_value, give_cols)

    @pl.loop(0, rows // LANES)
    def _(k):
        part = pl.ds(pl.multiple_of(k * LANES, LANES), LANES)
        merged = own
        for a in reversed(range(4)):
            ends = jnp.where(lane < LANES // 2, low[a, part, :], high[a, part, :])
            merged = jnp.where(lane < 8 * a + 8, pltpu.roll(ends, 8 * a + EDGE, 1), merged)
        packed[:, part] = merged.T[:6 * SUB, :]

    pl.semaphore_wait(barrier, devices - 1)
    mid = pl.ds(LANES, rows)
    start, end = pl.ds(0, LANES), pl.ds(rows - LANES, LANES)
    above, under = pl.ds(0, LANES), pl.ds(rows + LANES, LANES)
    plan = [
        (near, got_bottom), (far, got_top), (packed, got_right.at[:, mid]), (packed, got_left.at[:, mid]),
        (packed.at[:, start], got_right.at[:, under]), (packed.at[:, start], got_left.at[:, under]),
        (packed.at[:, end], got_right.at[:, above]), (packed.at[:, end], got_left.at[:, above]),
    ]
    halos = []
    for k, (move, (src, dst)) in enumerate(zip(moves, plan)):
        inside, device = there(*move)
        copy = pltpu.make_async_remote_copy(src, dst, halo_send.at[k], halo_recv.at[k], device_id=device,
                                            device_id_type=MESH)
        pl.when(inside)(copy.start)
        halos.append((inside, there(-move[0], -move[1])[0], copy))

    @pl.loop(1, windows)
    def _(s):
        all_loads(s, lambda copy: copy.start())

    w[...] = jnp.full(w.shape, wet_value)
    for copy in small[3:]:
        copy.wait()
    cell = cell_v[...]
    cell_row, cell_col = cell // width, cell % width
    turn = cell_row // SEG
    spot_v[...] = cell_col // LANES * tall + (windows - 1 - turn) * win + SUB + cell_row - turn * SEG
    to_scalar = pltpu.make_async_copy(spot_v, spot_s, small_sem.at[6])
    to_scalar.start()

    for sent, fed, copy in halos:
        pl.when(sent)(copy.wait_send)
        pl.when(fed)(copy.wait_recv)
    from_right = lax.broadcasted_iota(jnp.int32, (6 * SUB, LANES), 0) % SUB >= EDGE
    rest = jnp.zeros((LANES - 6 * SUB, LANES), jnp.float32)

    @pl.loop(0, rows // LANES + 2)
    def _(k):
        part = pl.ds(pl.multiple_of(k * LANES, LANES), LANES)
        both = jnp.where(from_right, got_right[:, part], got_left[:, part])
        side[part, :] = jnp.concatenate([both, rest], axis=0).T

    @pl.loop(0, windows)
    def _(s):
        mixed = side[pl.ds(pl.multiple_of((windows - 1 - s) * SEG + LANES - SUB, SUB), SEG + 16), :]
        at = pl.multiple_of(s * win, SUB)
        for a, dst in enumerate((d, g, f, c, w8)):
            base = (n - 1) * tall if a < 4 else 0
            dst[pl.ds(base + at, SEG + 16), :] = pltpu.roll(mixed, LANES - 8 * a - EDGE, 1)

    for a, (_, dst) in enumerate(arrays):
        for i in range(n - 1):
            lanes = pl.ds(i * LANES, LANES)
            dst[pl.ds(i * tall + (windows - 1) * win, SUB), :] = got_top[pl.ds(a * SUB, SUB), lanes]
            dst[pl.ds(i * tall + SEG + SUB, SUB), :] = got_bottom[pl.ds(a * SUB, SUB), lanes]
    w[pl.ds((windows - 1) * win, SUB), :] = got_top[pl.ds(4 * SUB, SUB), pl.ds(0, LANES)]
    w[pl.ds(SEG + SUB, SUB), :] = got_bottom[pl.ds(4 * SUB, SUB), pl.ds(0, LANES)]

    lane8 = lax.broadcasted_iota(jnp.int32, (SUB, LANES), 1)
    at_last, at_first = lane8 == LANES - 1, lane8 == 0
    at_top = lax.broadcasted_iota(jnp.int32, (SUB, LANES), 0) == 0

    def rightward(vals):
        rolled = [pltpu.roll(v, LANES - 1, 1) for v in vals]
        return [jnp.where(at_last, rolled[(i + 1) % n], rolled[i]) for i in range(n)]

    def leftward(vals):
        rolled = [pltpu.roll(v, 1, 1) for v in vals]
        return [jnp.where(at_first, rolled[(i - 1) % n], rolled[i]) for i in range(n)]

    def factors(r):
        vals = []
        for ref in (w, w8):
            v = ref[pl.ds(r, SUB), :]
            vals.append((gravity * time_step * v, gravity * time_step * friction * v, time_step * v))
        return [vals[0]] * (n - 1) + [vals[1]]

    def block(s, b, count, step, carry):
        base = s * win
        pairs = [(i, j) for j in range(count) for i in range(n)]
        rr = [pl.multiple_of(base + (b + j) * SUB, SUB) for j in range(count)]
        zz = [pl.multiple_of((b + j) * SUB, SUB) for j in range(count)]
        load = lambda ref, off=0: {(i, j): ref[pl.ds(i * tall + rr[j] + off, SUB), :] for i, j in pairs}
        local = lambda ref: {(i, j): ref[pl.ds(i * win + zz[j], SUB), :] for i, j in pairs}
        level, below = load(d), load(d, 1)
        if step == 0:
            bed, bed_below = load(g), load(g, 1)
        else:
            top_r, top_c = local(zr), local(zc)
            if step == STEPS - 1:
                bed = load(g)
        old_f, old_c = load(f), load(c)
        terms = [factors(r) for r in rr]
        carry = list(carry)
        done, tops = {}, {}
        for j in range(count):
            if step == 0:
                eta = [level[i, j] + bed[i, j] for i in range(n)]
                under_eta = [below[i, j] + bed_below[i, j] for i in range(n)]
                beds = [bed[i, j] for i in range(n)]
                rows_top = [jnp.maximum(beds[i], bed_below[i, j]) for i in range(n)]
                cols_top = [jnp.maximum(v, q) for v, q in zip(beds, rightward(beds))]
                for i in range(n):
                    tops[i, j] = rows_top[i], cols_top[i]
            else:
                eta = [level[i, j] for i in range(n)]
                under_eta = [below[i, j] for i in range(n)]
                rows_top = [top_r[i, j] for i in range(n)]
                cols_top = [top_c[i, j] for i in range(n)]
            right = rightward(eta)
            cols = [face_update(old_c[i, j], eta[i], right[i], cols_top[i], *terms[j][i][:2]) for i in range(n)]
            before = leftward(cols)
            for i in range(n if step < STEPS - 1 else n - 1):
                new = face_update(old_f[i, j], eta[i], under_eta[i], rows_top[i], *terms[j][i][:2])
                turned = pltpu.roll(new, 1, 0)
                up = jnp.where(at_top, carry[i], turned)
                carry[i] = turned
                moved = eta[i] + terms[j][i][2] * (up - new + before[i] - cols[i])
                if step == STEPS - 1:
                    moved = moved - bed[i, j]
                done[i, j] = (moved, new, cols[i])
        for (i, j), values in done.items():
            if step < STEPS - 1:
                for ref, value in zip((d, f, c), values):
                    ref[pl.ds(i * tall + rr[j], SUB), :] = value
            else:
                d[pl.ds(i * tall + rr[j], SUB), :] = values[0]
                at = pl.multiple_of((windows - 1 - s) * SEG + (b + j) * SUB - SUB, SUB)
                for a, value in enumerate(values):
                    fin[a, pl.ds(at, SUB), pl.ds(i * LANES, LANES)] = value
        for (i, j), values in tops.items():
            for ref, value in zip((zr, zc), values):
                ref[pl.ds(i * win + zz[j], SUB), :] = value
        return tuple(carry)

    def first_flow(s):
        r = pl.multiple_of(s * win, SUB)
        terms = factors(r)
        carry = []
        for i in range(n):
            eta, under_eta, old = (ref[pl.ds(i * tall + r + off, SUB), :] for ref, off in ((d, 0), (d, 1), (f, 0)))
            new = face_update(old, eta, under_eta, zr[pl.ds(i * win, SUB), :], *terms[i][:2])
            carry.append(pltpu.roll(new, 1, 0))
        return tuple(carry)

    def out_copies(s):
        at = pl.multiple_of((windows - 1 - s) * SEG, SEG)
        return [pltpu.make_async_copy(fin.at[a, pl.ds(at, SEG), :], ref.at[pl.ds(at, SEG), :], out_sem.at[a, s])
                for a, ref in enumerate((out_d, out_f, out_c))]

    def col_copies(s):
        at = pl.multiple_of((windows - 1 - s) * SEG, SEG)
        return [pltpu.make_async_remote_copy(
            fin.at[a, pl.ds(at, SEG), pl.ds(width - span, span)], moved_cols.at[a, pl.ds(at, SEG), :],
            col_send.at[a, s], col_recv.at[a, s], device_id=(me_row, me_col + 1), device_id_type=MESH)
            for a in range(3)]

    def row_copies(s):
        at = pl.multiple_of((windows - 1 - s) * SEG, SEG)
        to = pl.multiple_of(span - SEG - s * SEG, SEG)
        return [pltpu.make_async_remote_copy(
            fin.at[a, pl.ds(at, SEG), :], moved_rows.at[a, pl.ds(to, SEG), :],
            row_send.at[a, s], row_recv.at[a, s], device_id=(me_row + 1, me_col), device_id_type=MESH)
            for a in range(3)]

    gives_right, gives_down = me_col < n_col - 1, me_row < n_row - 1
    takes_left, takes_up = me_col > 0, me_row > 0
    blanks = (blank,) * n

    @pl.loop(0, windows)
    def _(s):
        all_loads(s, lambda copy: copy.wait())
        for step in range(2):
            lax.fori_loop(0, (SEG + 16) // SUB // GROUP, lambda k, old, step=step: block(s, k * GROUP, GROUP, step, old),
                          blanks)
        lax.fori_loop(0, SEG // SUB // GROUP, lambda k, old: block(s, k * GROUP + 1, GROUP, STEPS - 1, old), first_flow(s))

        @pl.when(gives_right)
        def _():
            for copy in col_copies(s):
                copy.start()

        @pl.when(jnp.logical_and(gives_down, s < span // SEG))
        def _():
            for copy in row_copies(s):
                copy.start()

        for copy in out_copies(s):
            copy.start()

    to_scalar.wait()

    @pl.loop(0, picked.shape[0] // 16)
    def _(k):
        row = k * 16 // LANES
        base = pl.multiple_of(k * 16, 16)
        for j in range(16):
            picked[pl.ds(base + j, 1), :] = d[pl.ds(spot_s[row, base - row * LANES + j], 1), :]

    acc[...] = jnp.zeros_like(acc)
    deep = lax.broadcasted_iota(jnp.int32, (LANES, LANES), 0)
    wide = lax.broadcasted_iota(jnp.int32, (devices, LANES), 0)

    @pl.loop(0, picked.shape[0] // LANES)
    def _(k):
        line = pl.ds(k, 1)
        chunk = picked[pl.ds(pl.multiple_of(k * LANES, LANES), LANES), :].T
        chosen = jnp.sum(jnp.where(deep == cell_v[line, :] % LANES, chunk, 0.0), axis=0, keepdims=True)
        captured = coef_v[line, :] * jnp.maximum(chosen, 0.0)
        node = node_v[line, :]
        owner = jnp.where(wide == node // NODE_DEV, captured, 0.0)
        within = (deep == node % NODE_DEV).astype(jnp.float32)
        acc[...] += lax.dot_general(owner, within, (((1,), (1,)), ((), ())), precision=lax.Precision.HIGHEST,
                                    preferred_element_type=jnp.float32)

    for k in range(devices):
        parts[k] = acc[pl.ds(k, 1), :]

    def send(k):
        other, device = place(k)
        return pltpu.make_async_remote_copy(parts.at[other], slots.at[k], node_send.at[k], node_recv.at[k],
                                            device_id=device, device_id_type=MESH)

    @pl.loop(1, devices)
    def _(k):
        send(k).start()

    @pl.loop(1, devices)
    def _(k):
        send(k).wait()

    note[pl.ds(0, 1), :] = parts[me] + jnp.sum(slots[pl.ds(1, devices - 1)], axis=0)
    note[pl.ds(1, 1), :] = got_top[pl.ds(5 * SUB, 1), pl.ds(0, LANES)]
    note[pl.ds(2, 1), :] = got_left[pl.ds(5 * SUB, 1), pl.ds(LANES, LANES)]
    note[pl.ds(3, 5), :] = jnp.zeros((5, LANES), jnp.float32)
    last = pltpu.make_async_copy(note, extra, small_sem.at[7])
    last.start()

    @pl.loop(0, windows)
    def _(s):
        for copy in out_copies(s):
            copy.wait()
        for copy in col_copies(s):
            pl.when(gives_right)(copy.wait_send)
            pl.when(takes_left)(copy.wait_recv)
        for copy in row_copies(s):
            pl.when(jnp.logical_and(gives_down, s < span // SEG))(copy.wait_send)
            pl.when(jnp.logical_and(takes_up, s < span // SEG))(copy.wait_recv)

    last.wait()


def fused(arrays, wet, shift_rows, shift_cols, cells, nodes, coefs):
    rows, width = arrays[0].shape
    counts = (lax.axis_size("row"), lax.axis_size("col"))
    devices = counts[0] * counts[1]
    span = MAX_BLOCKS * BLOCK
    n, windows, win = width // LANES + 1, rows // SEG, SEG + 24
    tall = windows * win
    lines = cells.shape[0]
    hbm, free = pl.BlockSpec(memory_space=pltpu.HBM), pl.BlockSpec(memory_space=pl.ANY)
    vmem = lambda *shape: pltpu.VMEM(shape, jnp.float32)
    sems = lambda *shape: pltpu.SemaphoreType.DMA(shape)
    across, along = (6 * SUB, width), (6 * SUB, rows + 2 * LANES)
    shapes = [(rows, width)] * 3 + [(3, span, width), (3, rows, span), (SUB, LANES)]
    state = vmem(n * tall, LANES)
    return pl.pallas_call(
        functools.partial(fused_kernel, counts),
        out_shape=[jax.ShapeDtypeStruct(shape, jnp.float32) for shape in shapes],
        in_specs=[hbm] * 10,
        out_specs=[free] * len(shapes),
        scratch_shapes=[
            state, state, state, state, vmem(tall, LANES), vmem(tall, LANES), vmem(n * win, LANES), vmem(n * win, LANES),
            vmem(3, rows, width), vmem(4, rows, LANES), vmem(4, rows, LANES), vmem(6 * SUB, rows),
            vmem(*across), vmem(*across), vmem(*across), vmem(*across), vmem(*along), vmem(*along),
            vmem(rows + 2 * LANES, LANES),
            pltpu.VMEM((lines, LANES), jnp.int32), pltpu.VMEM((lines, LANES), jnp.int32), vmem(lines, LANES),
            pltpu.VMEM((lines, LANES), jnp.int32), vmem(lines * LANES, LANES), vmem(devices, LANES),
            vmem(devices, 1, LANES), vmem(devices, 1, LANES), vmem(SUB, LANES),
            pltpu.SMEM((3, 1, 1), jnp.int32), pltpu.SMEM((lines, LANES), jnp.int32),
            sems(windows, 4, n), sems(4, 4), sems(8), sems(8), sems(8), sems(3, windows), sems(3, windows),
            sems(3, windows), sems(3, windows), sems(3, windows), sems(devices), sems(devices),
        ],
        compiler_params=pltpu.CompilerParams(collective_id=0, has_side_effects=True, vmem_limit_bytes=38 << 20),
        name="fused",
    )(*arrays, wet, shift_rows, shift_cols, cells, nodes, coefs)


def finish_kernel(d, f, c, rows_in, cols_in, extra, out_d, out_f, out_c, out_rows, out_cols, out_node,
                  zero_rows, zero_cols, note, sem, row_sem, col_sem, note_sem):
    fetch = pltpu.make_async_copy(extra, note, note_sem.at[0])
    fetch.start()
    copies = [pltpu.make_async_copy(src, dst, sem.at[a]) for a, (src, dst) in enumerate(
        ((d, out_d), (f, out_f), (c, out_c)))]
    for copy in copies:
        copy.start()
    zero_rows[...] = jnp.zeros_like(zero_rows)
    zero_cols[...] = jnp.zeros_like(zero_cols)
    fetch.wait()
    given_rows = jnp.max(note[pl.ds(1, 1), :])
    given_cols = jnp.max(note[pl.ds(2, 1), :])

    def hand_on(src, hole, dst, one, keep):
        copy = pltpu.make_async_copy(src, dst, one)
        fill = pltpu.make_async_copy(hole, dst, one)
        pl.when(keep)(copy.start)
        pl.when(jnp.logical_not(keep))(fill.start)
        copies.append(copy)

    for k in range(MAX_BLOCKS):
        part = pl.ds(k * BLOCK, BLOCK)
        for a in range(3):
            hand_on(rows_in.at[a, part, :], zero_rows, out_rows.at[a, part, :], row_sem.at[a, k],
                    given_rows >= MAX_BLOCKS - k)
            hand_on(cols_in.at[a, :, part], zero_cols, out_cols.at[a, :, part], col_sem.at[a, k],
                    given_cols >= MAX_BLOCKS - k)
    out_node[...] = note[pl.ds(0, 1), pl.ds(0, NODE_DEV)]
    for copy in copies:
        copy.wait()


def finish(d, f, c, moved_rows, moved_cols, extra):
    rows, width = d.shape
    free, hbm = pl.BlockSpec(memory_space=pl.ANY), pl.BlockSpec(memory_space=pltpu.HBM)
    shapes = [x.shape for x in (d, f, c, moved_rows, moved_cols)] + [(1, NODE_DEV)]
    return pl.pallas_call(
        finish_kernel,
        out_shape=[jax.ShapeDtypeStruct(shape, jnp.float32) for shape in shapes],
        in_specs=[free] * 6,
        out_specs=[hbm] * 5 + [pl.BlockSpec(memory_space=pltpu.VMEM)],
        scratch_shapes=[pltpu.VMEM((BLOCK, width), jnp.float32), pltpu.VMEM((rows, BLOCK), jnp.float32),
                        pltpu.VMEM((SUB, LANES), jnp.float32), pltpu.SemaphoreType.DMA((3,)),
                        pltpu.SemaphoreType.DMA((3, MAX_BLOCKS)), pltpu.SemaphoreType.DMA((3, MAX_BLOCKS)),
                        pltpu.SemaphoreType.DMA((1,))],
        compiler_params=pltpu.CompilerParams(vmem_limit_bytes=2 << 20),
        name="finish",
    )(d, f, c, moved_rows, moved_cols, extra)


def body(
    depth,
    ground,
    flow_rows,
    flow_cols,
    wet_tiles,
    inlet_cell,
    inlet_node,
    inlet_coef,
    shift_rows,
    shift_cols,
):
    flat = lambda x: x.reshape(-1, LANES)
    results = fused((depth, ground, flow_rows, flow_cols), wet_tiles, shift_rows, shift_cols,
                    flat(inlet_cell), flat(inlet_node), flat(inlet_coef))
    depth, flow_rows, flow_cols, moved_rows, moved_cols, node_inflow = finish(*results)
    return (depth, flow_rows, flow_cols, node_inflow[0], moved_rows, moved_cols)


def solution(mesh):
    return jax.shard_map(
        body,
        mesh=mesh,
        in_specs=(
            P("row", "col"),
            P("row", "col"),
            P("row", "col"),
            P("row", "col"),
            P("row", "col"),
            P("row", "col", None),
            P("row", "col", None),
            P("row", "col", None),
            P("row", "col"),
            P("row", "col"),
        ),
        out_specs=(
            P("row", "col"),
            P("row", "col"),
            P("row", "col"),
            P(("row", "col")),
            P(None, "row", "col"),
            P(None, "row", "col"),
        ),
        check_vma=False,
    )
```

```python
import functools

import jax
import jax.numpy as jnp
from jax import lax
from jax.experimental import pallas as pl
from jax.experimental.pallas import tpu as pltpu
from jax.sharding import PartitionSpec as P

STEPS = 3
BLOCK = 128
MAX_BLOCKS = 2
NODE_DEV = 64
LANES = 128
SUB = 8
EDGE = 4
GROUP = 2
EARLY_GROUP = 6
EARLY_LAST = 4
EARLY_NOW = 0
LINES = 4
SEG = 128
MESH = pl.DeviceIdType.MESH


gravity = 9.81
time_step = 0.1
friction = 0.0025
depth_floor = 0.25
POWER = -7.0 / 3.0


def face_update(flow, eta, eta_next, top, pull, rub):
    over = jnp.maximum(eta, eta_next) - top
    root = jnp.exp2(POWER * lax.log2(jnp.maximum(over, depth_floor)))
    drag = rub * jnp.abs(flow) * root
    pushed = flow - pull * jnp.maximum(over, 0.0) * (eta_next - eta)
    return pushed * pl.reciprocal(1.0 + drag)


def fused_kernel(counts, *refs):
    depth, ground, frow, fcol, flags, cells, nodes, coefs = refs[:8]
    out_d, out_f, out_c, moved_rows, moved_cols, extra = refs[8:14]
    (d, g, f, c, w, w8, zr, zc, fin, early_d, early_f, early_c, early_zr, early_zc, early, ship,
     pack_low, pack_high, first_rows, last_rows, near, far, got_top, got_bottom, got_left, got_right, side,
     flag_v, cell_v, node_v, coef_v, spot_v, picked, acc, parts, slots, note, spot_s,
     in_sem, edge_sem, small_sem, halo_send, halo_recv, out_sem, col_send, col_recv, row_send, row_recv,
     early_send, early_recv, node_send, node_recv) = refs[14:]
    n_row, n_col = counts
    devices = n_row * n_col
    rows, width = depth.shape
    n = width // LANES + 1
    windows = rows // SEG
    win = SEG + 24
    tall = windows * win
    span = MAX_BLOCKS * BLOCK
    near_right = (width - span) // LANES
    me_row, me_col = lax.axis_index("row"), lax.axis_index("col")
    me = me_row * n_col + me_col
    moves = [(-1, 0), (1, 0), (0, -1), (0, 1), (-1, -1), (-1, 1), (1, -1), (1, 1)]
    arrays = ((depth, d), (ground, g), (frow, f), (fcol, c))

    def place(k):
        other = lax.rem(me + k, devices)
        return other, (other // n_col, lax.rem(other, n_col))

    def there(dr, dc):
        r, q = me_row + dr, me_col + dc
        inside = jnp.logical_and(jnp.logical_and(r >= 0, r < n_row), jnp.logical_and(q >= 0, q < n_col))
        return inside, (r, q)

    for ref in (got_top, got_bottom, got_left, got_right):
        ref[...] = jnp.zeros_like(ref)
    barrier = pltpu.get_barrier_semaphore()

    @pl.loop(1, devices)
    def _(k):
        pl.semaphore_signal(barrier, inc=1, device_id=place(k)[1], device_id_type=MESH)

    small = [pltpu.make_async_copy(src, dst, small_sem.at[k]) for k, (src, dst) in enumerate((
        (flags, flag_v), (cells, cell_v), (nodes, node_v), (coefs, coef_v)))]
    small[0].start()
    edges = []
    for a, (src, _) in enumerate(arrays):
        for k, (piece, dst) in enumerate((
            (src.at[:, pl.ds(0, LANES)], picked.at[pl.ds(a * rows, rows)]),
            (src.at[:, pl.ds(width - LANES, LANES)], ship.at[pl.ds(a * rows, rows)]),
            (src.at[pl.ds(0, SUB), :], first_rows.at[pl.ds(a * SUB, SUB), :]),
            (src.at[pl.ds(rows - SUB, SUB), :], last_rows.at[pl.ds(a * SUB, SUB), :]),
        )):
            edges.append(pltpu.make_async_copy(piece, dst, edge_sem.at[a, k]))
            edges[-1].start()

    def loads(s, kind):
        lead, trail = (0 if kind == "top" else SUB), (0 if kind == "bottom" else SUB)
        start = (windows - 1 - s) * SEG - lead
        at = s * win + SUB - lead
        if not isinstance(s, int):
            start, at = pl.multiple_of(start, SUB), pl.multiple_of(at, SUB)
        high_rows = SEG + lead + trail
        return [pltpu.make_async_copy(src.at[pl.ds(start, high_rows), pl.ds(i * LANES, LANES)],
                                      dst.at[pl.ds(i * tall + at, high_rows)], in_sem.at[s, a, i])
                for a, (src, dst) in enumerate(arrays) for i in range(n - 1)]

    for copy in loads(1, "middle"):
        copy.start()

    blank = jnp.zeros((SUB, LANES), jnp.float32)
    for buf in (d, g):
        for i in range(n):
            for s in range(windows):
                buf[pl.ds(i * tall + s * win + SEG + 16, SUB), :] = blank
    for i in range(3):
        early_d[pl.ds(i * win + SEG + 16, SUB), :] = blank
    small[0].wait()
    wet_value = jnp.broadcast_to(flag_v[pl.ds(0, 1), :], (SUB, LANES))
    row8 = lax.broadcasted_iota(jnp.int32, (SUB, LANES), 0)
    upper = row8 < EDGE
    marks = [jnp.where(upper, wet_value, jnp.broadcast_to(flag_v[pl.ds(k, 1), :], (SUB, LANES))) for k in (1, 2)]
    turn4 = lambda v: pltpu.roll(v, EDGE, 0)
    for copy in edges:
        copy.wait()
    for i in range(n - 1):
        lanes = pl.ds(i * LANES, LANES)
        for m in range(2):
            part = pl.ds(m * SUB, SUB)
            one, two = pl.ds(2 * m * SUB, SUB), pl.ds((2 * m + 1) * SUB, SUB)
            near[part, lanes] = jnp.where(upper, first_rows[one, lanes], turn4(first_rows[two, lanes]))
            far[part, lanes] = jnp.where(upper, turn4(last_rows[one, lanes]), last_rows[two, lanes])
        near[pl.ds(2 * SUB, SUB), lanes] = marks[0]
        far[pl.ds(2 * SUB, SUB), lanes] = marks[0]
    lane = lax.broadcasted_iota(jnp.int32, (LANES, LANES), 1)

    @pl.loop(0, rows // LANES)
    def _(k):
        part = pl.ds(pl.multiple_of(k * LANES, LANES), LANES)
        merged = None
        for a in reversed(range(4)):
            at = pl.ds(pl.multiple_of(a * rows + k * LANES, LANES), LANES)
            ends = jnp.where(lane < LANES // 2, picked[at, :], ship[at, :])
            turned = pltpu.roll(ends, 8 * a + EDGE, 1)
            merged = turned if merged is None else jnp.where(lane < 8 * a + 8, turned, merged)
        lines = merged.T[:4 * SUB, :]
        group = [lines[a * SUB:(a + 1) * SUB, :] for a in range(4)]
        for m in range(2):
            one, two = group[2 * m], group[2 * m + 1]
            pack_low[pl.ds(m * SUB, SUB), part] = jnp.where(upper, turn4(one), two)
            pack_high[pl.ds(m * SUB, SUB), part] = jnp.where(upper, one, turn4(two))
        pack_low[pl.ds(2 * SUB, SUB), part] = marks[1]
        pack_high[pl.ds(2 * SUB, SUB), part] = marks[1]

    pl.semaphore_wait(barrier, devices - 1)
    mid = pl.ds(LANES, rows)
    start, end = pl.ds(0, LANES), pl.ds(rows - LANES, LANES)
    above, under = pl.ds(0, LANES), pl.ds(rows + LANES, LANES)
    plan = [
        (near, got_bottom), (far, got_top), (pack_low, got_right.at[:, mid]), (pack_high, got_left.at[:, mid]),
        (pack_low.at[:, start], got_right.at[:, under]), (pack_high.at[:, start], got_left.at[:, under]),
        (pack_low.at[:, end], got_right.at[:, above]), (pack_high.at[:, end], got_left.at[:, above]),
    ]
    halos = []
    for k, (move, (src, dst)) in enumerate(zip(moves, plan)):
        inside, device = there(*move)
        copy = pltpu.make_async_remote_copy(src, dst, halo_send.at[k], halo_recv.at[k], device_id=device,
                                            device_id_type=MESH)
        pl.when(inside)(copy.start)
        halos.append((inside, there(-move[0], -move[1])[0], copy))

    @pl.loop(2, windows - 1)
    def _(s):
        for copy in loads(s, "middle"):
            copy.start()

    for copy in loads(0, "bottom") + loads(windows - 1, "top") + small[1:]:
        copy.start()

    lane8 = lax.broadcasted_iota(jnp.int32, (SUB, LANES), 1)
    at_last, at_first = lane8 == LANES - 1, lane8 == 0
    at_top = row8 == 0

    def rightward(vals):
        rolled = [pltpu.roll(v, LANES - 1, 1) for v in vals]
        return [jnp.where(at_last, rolled[(i + 1) % len(vals)], rolled[i]) for i in range(len(vals))]

    def leftward(vals):
        rolled = [pltpu.roll(v, 1, 1) for v in vals]
        return [jnp.where(at_first, rolled[i - 1], rolled[i]) for i in range(len(vals))]

    def scaled(v):
        return gravity * time_step * v, gravity * time_step * friction * v, time_step * v

    def factors(r):
        return [scaled(w[pl.ds(r, SUB), :])] * (n - 1) + [scaled(w8[pl.ds(r, SUB), :])]

    def update(eta, under_eta, tops, old_f, old_c, terms, carry, wanted):
        right = rightward(eta)
        cols = [face_update(old_c[i], eta[i], right[i], tops[1][i], *terms[i][:2]) for i in range(len(eta))]
        before = leftward(cols)
        carry, done = list(carry), {}
        for i in wanted:
            new = face_update(old_f[i], eta[i], under_eta[i], tops[0][i], *terms[i][:2])
            turned = pltpu.roll(new, 1, 0)
            up = jnp.where(at_top, carry[i], turned)
            carry[i] = turned
            done[i] = (eta[i] + terms[i][2] * (up - new + before[i] - cols[i]), new, cols[i])
        return done, carry

    def block(s, b, count, step, carry, slabs, state, tops, terms_of, wanted, store):
        m = len(slabs)
        at = [pl.multiple_of(s * win + (b + j) * SUB, SUB) for j in range(count)]
        zz = [pl.multiple_of((b + j) * SUB, SUB) for j in range(count)]
        own = state[0] is d
        wide_at = lambda i, j: slabs[i] * tall + at[j]
        here = wide_at if own else (lambda i, j: i * win + zz[j])
        source = (d, f, c) if step == 0 else state
        spot = wide_at if step == 0 else here
        pull = lambda ref, where, off=0: [[ref[pl.ds(where(i, j) + off, SUB), :] for i in range(m)] for j in range(count)]
        level, below = pull(source[0], spot), pull(source[0], spot, 1)
        old_f, old_c = pull(source[1], spot), pull(source[2], spot)
        if step == 0:
            bed, bed_below = pull(g, wide_at), pull(g, wide_at, 1)
        else:
            faces = [pull(ref, lambda i, j: i * win + zz[j]) for ref in tops]
        terms = [terms_of(r) for r in at]
        if step == STEPS - 1:
            floor = [{i: g[pl.ds(wide_at(i, j), SUB), :] for i in wanted} for j in range(count)]
        writes = []
        for j in range(count):
            eta, under_eta = level[j], below[j]
            if step == 0:
                eta = [x + y for x, y in zip(eta, bed[j])]
                under_eta = [x + y for x, y in zip(under_eta, bed_below[j])]
                face = ([jnp.maximum(x, y) for x, y in zip(bed[j], bed_below[j])],
                        [jnp.maximum(x, y) for x, y in zip(bed[j], rightward(bed[j]))])
                for ref, values in zip(tops, face):
                    for i in range(m):
                        writes.append((ref, i * win + zz[j], values[i]))
            else:
                face = (faces[0][j], faces[1][j])
            done, carry = update(eta, under_eta, face, old_f[j], old_c[j], terms[j], carry, wanted)
            for i, values in done.items():
                if step < STEPS - 1:
                    for ref, value in zip(state, values):
                        writes.append((ref, here(i, j), value))
                else:
                    done[i] = (values[0] - floor[j][i], values[1], values[2])
            if step == STEPS - 1:
                writes.append((None, j, done))
        for ref, where, value in writes:
            if ref is None:
                store(s, b + where, value)
            else:
                ref[pl.ds(where, SUB), :] = value
        return tuple(carry)

    def first_flow(s, slabs, state, top_rows, terms_of, wanted):
        r = pl.multiple_of(s * win, SUB)
        terms = terms_of(r)
        carry = []
        for i in range(len(slabs)):
            if i not in wanted:
                carry.append(blank)
                continue
            at = slabs[i] * tall + r if state[0] is d else i * win
            eta, under_eta, old = (ref[pl.ds(at + off, SUB), :] for ref, off in ((state[0], 0), (state[0], 1), (state[1], 0)))
            new = face_update(old, eta, under_eta, top_rows[pl.ds(i * win, SUB), :], *terms[i][:2])
            carry.append(pltpu.roll(new, 1, 0))
        return tuple(carry)

    def window(s, slabs, state, tops, terms_of, wanted, store, group, last_group):
        every = tuple(range(len(slabs)))
        for step in range(STEPS - 1):
            lax.fori_loop(0, (SEG + 16) // SUB // group, lambda k, old, step=step: block(
                s, k * group, group, step, old, slabs, state, tops, terms_of, every, store), (blank,) * len(slabs))
        lax.fori_loop(0, SEG // SUB // last_group, lambda k, old: block(
            s, k * last_group + 1, last_group, STEPS - 1, old, slabs, state, tops, terms_of, wanted, store),
            first_flow(s, slabs, state, tops[0], terms_of, wanted))

    gives_right, gives_down = me_col < n_col - 1, me_row < n_row - 1
    takes_left, takes_up = me_col > 0, me_row > 0
    own_terms = [scaled(wet_value)] * 3

    def store_early(s, b, done):
        at = pl.multiple_of(b * SUB - SUB, SUB)
        for a, value in enumerate(done[1]):
            early[s - 1, a, pl.ds(at, SUB), :] = value

    def early_copies(s):
        at = pl.multiple_of((windows - 1 - s) * SEG, SEG)
        return [pltpu.make_async_remote_copy(
            early.at[s - 1, a], moved_cols.at[a, pl.ds(at, SEG)],
            early_send.at[a, s], early_recv.at[a, s], device_id=(me_row, me_col + 1), device_id_type=MESH)
            for a in range(3)]

    @pl.loop(1, windows - 1)
    def _(s):
        for copy in loads(s, "middle"):
            copy.wait()
        window(s, [near_right - 1, near_right, near_right + 1], (early_d, early_f, early_c), (early_zr, early_zc),
               lambda r: own_terms, (1,), store_early, EARLY_GROUP, EARLY_LAST)

        @pl.when(jnp.logical_and(gives_right, s < 1 + EARLY_NOW))
        def _():
            for copy in early_copies(s):
                copy.start()

    w[...] = jnp.broadcast_to(flag_v[pl.ds(0, 1), :], w.shape)
    for copy in small[1:]:
        copy.wait()
    cell = cell_v[...]
    cell_row, cell_col = cell // width, cell % width
    turn = cell_row // SEG
    spot_v[...] = cell_col // LANES * tall + (windows - 1 - turn) * win + SUB + cell_row - turn * SEG
    to_scalar = pltpu.make_async_copy(spot_v, spot_s, small_sem.at[4])
    to_scalar.start()

    for sent, fed, copy in halos:
        pl.when(sent)(copy.wait_send)
        pl.when(fed)(copy.wait_recv)

    @pl.loop(1 + EARLY_NOW, windows - 1)
    def _(s):
        @pl.when(gives_right)
        def _():
            for copy in early_copies(s):
                copy.start()

    rest = jnp.zeros((LANES - 5 * SUB, LANES), jnp.float32)

    @pl.loop(0, rows // LANES + 2)
    def _(k):
        part = pl.ds(pl.multiple_of(k * LANES, LANES), LANES)
        both = []
        for m in range(3):
            left, right = (ref[pl.ds(m * SUB, SUB), part] for ref in (got_left, got_right))
            both.append(jnp.where(upper, left, turn4(right)))
            both.append(jnp.where(upper, turn4(left), right))
        side[part, :] = jnp.concatenate(both[:5] + [rest], axis=0).T

    @pl.loop(0, windows)
    def _(s):
        mixed = side[pl.ds(pl.multiple_of((windows - 1 - s) * SEG + LANES - SUB, SUB), SEG + 16), :]
        at = pl.multiple_of(s * win, SUB)
        for a, dst in enumerate((d, g, f, c, w8)):
            base = (n - 1) * tall if a < 4 else 0
            dst[pl.ds(base + at, SEG + 16), :] = pltpu.roll(mixed, LANES - 8 * a - EDGE, 1)

    for a, (_, dst) in enumerate(arrays):
        for i in range(n - 1):
            lanes = pl.ds(i * LANES, LANES)
            top, under = (ref[pl.ds(a // 2 * SUB, SUB), lanes] for ref in (got_top, got_bottom))
            dst[pl.ds(i * tall + (windows - 1) * win, SUB), :] = top if a % 2 else turn4(top)
            dst[pl.ds(i * tall + SEG + SUB, SUB), :] = turn4(under) if a % 2 else under
    w[pl.ds((windows - 1) * win, SUB), :] = turn4(got_top[pl.ds(2 * SUB, SUB), pl.ds(0, LANES)])
    w[pl.ds(SEG + SUB, SUB), :] = got_bottom[pl.ds(2 * SUB, SUB), pl.ds(0, LANES)]

    def store_main(s, b, done):
        at = pl.multiple_of((windows - 1 - s) * SEG + b * SUB - SUB, SUB)
        for i, values in done.items():
            d[pl.ds(pl.multiple_of(i * tall + s * win + b * SUB, SUB), SUB), :] = values[0]
            for a, value in enumerate(values):
                fin[a, pl.ds(at, SUB), pl.ds(i * LANES, LANES)] = value
                if i >= near_right:
                    ship[pl.ds(pl.multiple_of(((i - near_right) * 3 + a) * rows + at, SUB), SUB), :] = value

    def out_copies(s):
        at = pl.multiple_of((windows - 1 - s) * SEG, SEG)
        return [pltpu.make_async_copy(fin.at[a, pl.ds(at, SEG), :], ref.at[pl.ds(at, SEG), :], out_sem.at[a, s])
                for a, ref in enumerate((out_d, out_f, out_c))]

    def col_copies(s, k):
        at = pl.multiple_of((windows - 1 - s) * SEG, SEG)
        return [pltpu.make_async_remote_copy(
            ship.at[pl.ds(pl.multiple_of((k * 3 + a) * rows + at, SEG), SEG)], moved_cols.at[k * 3 + a, pl.ds(at, SEG)],
            col_send.at[k * 3 + a, s], col_recv.at[k * 3 + a, s], device_id=(me_row, me_col + 1), device_id_type=MESH)
            for a in range(3)]

    def row_copies(s):
        at = pl.multiple_of((windows - 1 - s) * SEG, SEG)
        to = pl.multiple_of(span - SEG - s * SEG, SEG)
        return [pltpu.make_async_remote_copy(
            fin.at[a, pl.ds(at, SEG), :], moved_rows.at[a, pl.ds(to, SEG), :],
            row_send.at[a, s], row_recv.at[a, s], device_id=(me_row + 1, me_col), device_id_type=MESH)
            for a in range(3)]

    def outer(s):
        return jnp.logical_or(s == 0, s == windows - 1)

    @pl.loop(0, windows)
    def _(s):
        for kind, index in (("bottom", 0), ("top", windows - 1)):
            @pl.when(s == index)
            def _():
                for copy in loads(index, kind):
                    copy.wait()

        window(s, list(range(n)), (d, f, c), (zr, zc), factors, tuple(range(n - 1)), store_main, GROUP, GROUP)
        for k, holds in ((0, outer(s)), (1, True)):
            @pl.when(jnp.logical_and(gives_right, holds))
            def _():
                for copy in col_copies(s, k):
                    copy.start()

        @pl.when(jnp.logical_and(gives_down, s < span // SEG))
        def _():
            for copy in row_copies(s):
                copy.start()

        for copy in out_copies(s):
            copy.start()

    to_scalar.wait()

    @pl.loop(0, picked.shape[0] // 16)
    def _(k):
        row = k * 16 // LANES
        base = pl.multiple_of(k * 16, 16)
        for j in range(16):
            picked[pl.ds(base + j, 1), :] = d[pl.ds(spot_s[row, base - row * LANES + j], 1), :]

    acc[...] = jnp.zeros_like(acc)
    deep = lax.broadcasted_iota(jnp.int32, (LANES, LANES), 0)
    wide = lax.broadcasted_iota(jnp.int32, (devices, LANES), 0)

    @pl.loop(0, picked.shape[0] // LANES // LINES)
    def _(k):
        total = acc[...]
        for j in range(LINES):
            line = pl.ds(k * LINES + j, 1)
            chunk = picked[pl.ds(pl.multiple_of((k * LINES + j) * LANES, LANES), LANES), :].T
            chosen = jnp.sum(jnp.where(deep == cell_v[line, :] % LANES, chunk, 0.0), axis=0, keepdims=True)
            captured = coef_v[line, :] * jnp.maximum(chosen, 0.0)
            node = node_v[line, :]
            mine = wide == node // NODE_DEV
            pieces = []
            for _ in range(3):
                piece = captured.astype(jnp.bfloat16).astype(jnp.float32)
                pieces.append(jnp.where(mine, piece, 0.0).astype(jnp.bfloat16))
                captured = captured - piece
            within = (deep == node % NODE_DEV).astype(jnp.bfloat16)
            total = total + lax.dot_general(jnp.concatenate(pieces, axis=0), within, (((1,), (1,)), ((), ())),
                                            preferred_element_type=jnp.float32)
        acc[...] = total

    for k in range(devices):
        parts[k] = acc[pl.ds(k, 1), :] + acc[pl.ds(devices + k, 1), :] + acc[pl.ds(2 * devices + k, 1), :]

    def send(k):
        other, device = place(k)
        return pltpu.make_async_remote_copy(parts.at[other], slots.at[k], node_send.at[k], node_recv.at[k],
                                            device_id=device, device_id_type=MESH)

    @pl.loop(1, devices)
    def _(k):
        send(k).start()

    @pl.loop(1, devices)
    def _(k):
        send(k).wait()

    note[pl.ds(0, 1), :] = parts[me] + jnp.sum(slots[pl.ds(1, devices - 1)], axis=0)
    note[pl.ds(1, 1), :] = got_top[pl.ds(2 * SUB + EDGE, 1), pl.ds(0, LANES)]
    note[pl.ds(2, 1), :] = got_left[pl.ds(2 * SUB + EDGE, 1), pl.ds(LANES, LANES)]
    note[pl.ds(3, 5), :] = jnp.zeros((5, LANES), jnp.float32)
    last = pltpu.make_async_copy(note, extra, small_sem.at[5])
    last.start()

    @pl.loop(0, windows)
    def _(s):
        for copy in out_copies(s):
            copy.wait()
        for some, holds in ((col_copies(s, 0), outer(s)), (col_copies(s, 1), True),
                            (early_copies(s), jnp.logical_not(outer(s)))):
            for copy in some:
                pl.when(jnp.logical_and(gives_right, holds))(copy.wait_send)
                pl.when(jnp.logical_and(takes_left, holds))(copy.wait_recv)
        for copy in row_copies(s):
            pl.when(jnp.logical_and(gives_down, s < span // SEG))(copy.wait_send)
            pl.when(jnp.logical_and(takes_up, s < span // SEG))(copy.wait_recv)

    last.wait()


def fused(arrays, flags, cells, nodes, coefs):
    rows, width = arrays[0].shape
    counts = (lax.axis_size("row"), lax.axis_size("col"))
    devices = counts[0] * counts[1]
    span = MAX_BLOCKS * BLOCK
    n, windows, win = width // LANES + 1, rows // SEG, SEG + 24
    tall = windows * win
    lines = cells.shape[0]
    hbm, free = pl.BlockSpec(memory_space=pltpu.HBM), pl.BlockSpec(memory_space=pl.ANY)
    vmem = lambda *shape: pltpu.VMEM(shape, jnp.float32)
    sems = lambda *shape: pltpu.SemaphoreType.DMA(shape)
    across, along = (3 * SUB, width), (3 * SUB, rows + 2 * LANES)
    raw, part = (4 * SUB, width), (3 * win, LANES)
    shapes = [(rows, width)] * 3 + [(3, span, width), (3 * MAX_BLOCKS, rows, LANES), (SUB, LANES)]
    state = vmem(n * tall, LANES)
    return pl.pallas_call(
        functools.partial(fused_kernel, counts),
        out_shape=[jax.ShapeDtypeStruct(shape, jnp.float32) for shape in shapes],
        in_specs=[hbm] * 4 + [free] + [hbm] * 3,
        out_specs=[free] * len(shapes),
        scratch_shapes=[
            state, state, state, state, vmem(tall, LANES), vmem(tall, LANES), vmem(n * win, LANES), vmem(n * win, LANES),
            vmem(3, rows, width), vmem(*part), vmem(*part), vmem(*part), vmem(*part), vmem(*part),
            vmem(windows - 2, 3, SEG, LANES), vmem(3 * MAX_BLOCKS * rows, LANES), vmem(3 * SUB, rows),
            vmem(3 * SUB, rows), vmem(*raw), vmem(*raw), vmem(*across), vmem(*across), vmem(*across), vmem(*across),
            vmem(*along), vmem(*along), vmem(rows + 2 * LANES, LANES), vmem(SUB, LANES),
            pltpu.VMEM((lines, LANES), jnp.int32), pltpu.VMEM((lines, LANES), jnp.int32), vmem(lines, LANES),
            pltpu.VMEM((lines, LANES), jnp.int32), vmem(lines * LANES, LANES), vmem(3 * devices, LANES),
            vmem(devices, 1, LANES), vmem(devices, 1, LANES), vmem(SUB, LANES), pltpu.SMEM((lines, LANES), jnp.int32),
            sems(windows, 4, n), sems(4, 4), sems(8), sems(8), sems(8), sems(3, windows), sems(6, windows),
            sems(6, windows), sems(3, windows), sems(3, windows), sems(3, windows), sems(3, windows), sems(devices),
            sems(devices),
        ],
        compiler_params=pltpu.CompilerParams(collective_id=0, has_side_effects=True, vmem_limit_bytes=38 << 20),
        name="fused",
    )(*arrays, flags, *[pltpu.with_memory_space_constraint(x, pltpu.HBM) for x in (cells, nodes, coefs)])


def finish_kernel(d, f, c, rows_in, cols_in, extra, out_d, out_f, out_c, out_rows, out_cols, out_node,
                  zero_rows, zero_cols, note, sem, row_sem, col_sem, note_sem):
    fetch = pltpu.make_async_copy(extra, note, note_sem.at[0])
    fetch.start()
    copies = [pltpu.make_async_copy(src, dst, sem.at[a]) for a, (src, dst) in enumerate(
        ((d, out_d), (f, out_f), (c, out_c)))]
    for copy in copies:
        copy.start()
    zero_rows[...] = jnp.zeros_like(zero_rows)
    zero_cols[...] = jnp.zeros_like(zero_cols)
    fetch.wait()
    given_rows = jnp.max(note[pl.ds(1, 1), :])
    given_cols = jnp.max(note[pl.ds(2, 1), :])

    def hand_on(src, hole, dst, one, keep):
        copy = pltpu.make_async_copy(src, dst, one)
        fill = pltpu.make_async_copy(hole, dst, one)
        pl.when(keep)(copy.start)
        pl.when(jnp.logical_not(keep))(fill.start)
        copies.append(copy)

    for k in range(MAX_BLOCKS):
        part = pl.ds(k * BLOCK, BLOCK)
        for a in range(3):
            hand_on(rows_in.at[a, part, :], zero_rows, out_rows.at[a, part, :], row_sem.at[a, k],
                    given_rows >= MAX_BLOCKS - k)
            hand_on(cols_in.at[k * 3 + a], zero_cols, out_cols.at[a, :, part], col_sem.at[a, k],
                    given_cols >= MAX_BLOCKS - k)
    out_node[...] = note[pl.ds(0, 1), pl.ds(0, NODE_DEV)]
    for copy in copies:
        copy.wait()


def finish(d, f, c, moved_rows, moved_cols, extra):
    rows, width = d.shape
    free, hbm = pl.BlockSpec(memory_space=pl.ANY), pl.BlockSpec(memory_space=pltpu.HBM)
    shapes = [x.shape for x in (d, f, c, moved_rows)] + [(3, rows, MAX_BLOCKS * BLOCK), (1, NODE_DEV)]
    return pl.pallas_call(
        finish_kernel,
        out_shape=[jax.ShapeDtypeStruct(shape, jnp.float32) for shape in shapes],
        in_specs=[free] * 6,
        out_specs=[hbm] * 5 + [pl.BlockSpec(memory_space=pltpu.VMEM)],
        scratch_shapes=[pltpu.VMEM((BLOCK, width), jnp.float32), pltpu.VMEM((rows, BLOCK), jnp.float32),
                        pltpu.VMEM((SUB, LANES), jnp.float32), pltpu.SemaphoreType.DMA((3,)),
                        pltpu.SemaphoreType.DMA((3, MAX_BLOCKS)), pltpu.SemaphoreType.DMA((3, MAX_BLOCKS)),
                        pltpu.SemaphoreType.DMA((1,))],
        compiler_params=pltpu.CompilerParams(vmem_limit_bytes=2 << 20),
        name="finish",
    )(d, f, c, moved_rows, moved_cols, extra)


def body(
    depth,
    ground,
    flow_rows,
    flow_cols,
    wet_tiles,
    inlet_cell,
    inlet_node,
    inlet_coef,
    shift_rows,
    shift_cols,
):
    flat = lambda x: x.reshape(-1, LANES)
    line = lax.broadcasted_iota(jnp.int32, (SUB, LANES), 0)
    flags = jnp.where(line == 0, wet_tiles, jnp.where(line == 1, shift_rows, shift_cols)).astype(jnp.float32)
    results = fused((depth, ground, flow_rows, flow_cols), flags,
                    flat(inlet_cell), flat(inlet_node), flat(inlet_coef))
    depth, flow_rows, flow_cols, moved_rows, moved_cols, node_inflow = finish(*results)
    return (depth, flow_rows, flow_cols, node_inflow[0], moved_rows, moved_cols)


def solution(mesh):
    return jax.shard_map(
        body,
        mesh=mesh,
        in_specs=(
            P("row", "col"),
            P("row", "col"),
            P("row", "col"),
            P("row", "col"),
            P("row", "col"),
            P("row", "col", None),
            P("row", "col", None),
            P("row", "col", None),
            P("row", "col"),
            P("row", "col"),
        ),
        out_specs=(
            P("row", "col"),
            P("row", "col"),
            P("row", "col"),
            P(("row", "col")),
            P(None, "row", "col"),
            P(None, "row", "col"),
        ),
        check_vma=False,
    )
```

```python
import functools

import jax
import jax.numpy as jnp
from jax import lax
from jax.experimental import pallas as pl
from jax.experimental.pallas import tpu as pltpu
from jax.sharding import PartitionSpec as P

STEPS = 3
BLOCK = 128
MAX_BLOCKS = 2
NODE_DEV = 64
LANES = 128
SUB = 8
EDGE = 4
GROUP = 3
EARLY_GROUP = 6
EARLY_LAST = 4
EARLY_NOW = 0
EARLY = 2
LAST = 4
HELD = 1
LINES = 4
SEG = 128
MESH = pl.DeviceIdType.MESH


gravity = 9.81
time_step = 0.1
friction = 0.0025
depth_floor = 0.25
POWER = -7.0 / 3.0


def face_update(flow, eta, eta_next, top, pull, rub):
    over = jnp.maximum(eta, eta_next) - top
    root = jnp.exp2(POWER * lax.log2(jnp.maximum(over, depth_floor)))
    drag = rub * jnp.abs(flow) * root
    pushed = flow - pull * jnp.maximum(over, 0.0) * (eta_next - eta)
    return pushed * pl.reciprocal(1.0 + drag)


def fused_kernel(counts, *refs):
    depth, ground, frow, fcol, flags, cells, nodes, coefs = refs[:8]
    out_d, out_f, out_c, moved_rows, moved_cols, extra = refs[8:14]
    (d, g, f, c, w, w8, zr, zc, fin, early_d, early_f, early_c, early_zr, early_zc, early, ship,
     pack_low, pack_high, first_rows, last_rows, near, far, got_top, got_bottom, got_left, got_right, side,
     flag_v, cell_v, node_v, coef_v, spot_v, picked, acc, parts, slots, note, spot_s,
     in_sem, edge_sem, small_sem, halo_send, halo_recv, out_sem, col_send, col_recv, row_send, row_recv,
     early_send, early_recv, node_send, node_recv, spot_sem) = refs[14:]
    n_row, n_col = counts
    devices = n_row * n_col
    rows, width = depth.shape
    n = width // LANES + 1
    windows = rows // SEG
    win = SEG + 24
    tall = windows * win
    span = MAX_BLOCKS * BLOCK
    near_right = (width - span) // LANES
    me_row, me_col = lax.axis_index("row"), lax.axis_index("col")
    me = me_row * n_col + me_col
    moves = [(-1, 0), (1, 0), (0, -1), (0, 1), (-1, -1), (-1, 1), (1, -1), (1, 1)]
    arrays = ((depth, d), (ground, g), (frow, f), (fcol, c))

    def place(k):
        other = lax.rem(me + k, devices)
        return other, (other // n_col, lax.rem(other, n_col))

    def there(dr, dc):
        r, q = me_row + dr, me_col + dc
        inside = jnp.logical_and(jnp.logical_and(r >= 0, r < n_row), jnp.logical_and(q >= 0, q < n_col))
        return inside, (r, q)

    for ref in (got_top, got_bottom, got_left, got_right):
        ref[...] = jnp.zeros_like(ref)
    barrier = pltpu.get_barrier_semaphore()

    @pl.loop(1, devices)
    def _(k):
        pl.semaphore_signal(barrier, inc=1, device_id=place(k)[1], device_id_type=MESH)

    small = [pltpu.make_async_copy(src, dst, small_sem.at[k]) for k, (src, dst) in enumerate((
        (flags, flag_v), (cells, cell_v), (nodes, node_v), (coefs, coef_v)))]
    small[0].start()
    edges = []
    for a, (src, _) in enumerate(arrays):
        for k, (piece, dst) in enumerate((
            (src.at[:, pl.ds(0, LANES)], picked.at[pl.ds(a * rows, rows)]),
            (src.at[:, pl.ds(width - LANES, LANES)], ship.at[pl.ds(a * rows, rows)]),
            (src.at[pl.ds(0, SUB), :], first_rows.at[pl.ds(a * SUB, SUB), :]),
            (src.at[pl.ds(rows - SUB, SUB), :], last_rows.at[pl.ds(a * SUB, SUB), :]),
        )):
            edges.append(pltpu.make_async_copy(piece, dst, edge_sem.at[a, k]))
            edges[-1].start()

    def loads(s, kind):
        lead, trail = (0 if kind == "top" else SUB), (0 if kind == "bottom" else SUB)
        start = (windows - 1 - s) * SEG - lead
        at = s * win + SUB - lead
        if not isinstance(s, int):
            start, at = pl.multiple_of(start, SUB), pl.multiple_of(at, SUB)
        high_rows = SEG + lead + trail
        return [pltpu.make_async_copy(src.at[pl.ds(start, high_rows), pl.ds(i * LANES, LANES)],
                                      dst.at[pl.ds(i * tall + at, high_rows)], in_sem.at[s, a, i])
                for a, (src, dst) in enumerate(arrays) for i in range(n - 1)]

    for copy in loads(1, "middle"):
        copy.start()

    blank = jnp.zeros((SUB, LANES), jnp.float32)
    for buf in (d, g):
        for i in range(n):
            for s in range(windows):
                buf[pl.ds(i * tall + s * win + SEG + 16, SUB), :] = blank
    for i in range(3):
        early_d[pl.ds(i * win + SEG + 16, SUB), :] = blank
    small[0].wait()
    flag = lambda k: jnp.broadcast_to(jnp.broadcast_to(flag_v[pl.ds(k, 1), :][:, :1], (1, LANES)), (SUB, LANES))
    wet_value = flag(0)
    row8 = lax.broadcasted_iota(jnp.int32, (SUB, LANES), 0)
    upper = row8 < EDGE
    marks = [jnp.where(upper, wet_value, flag(k)) for k in (1, 2)]
    turn4 = lambda v: pltpu.roll(v, EDGE, 0)
    for copy in edges:
        copy.wait()
    for i in range(n - 1):
        lanes = pl.ds(i * LANES, LANES)
        for m in range(2):
            part = pl.ds(m * SUB, SUB)
            one, two = pl.ds(2 * m * SUB, SUB), pl.ds((2 * m + 1) * SUB, SUB)
            near[part, lanes] = jnp.where(upper, first_rows[one, lanes], turn4(first_rows[two, lanes]))
            far[part, lanes] = jnp.where(upper, turn4(last_rows[one, lanes]), last_rows[two, lanes])
        near[pl.ds(2 * SUB, SUB), lanes] = marks[0]
        far[pl.ds(2 * SUB, SUB), lanes] = marks[0]
    lane = lax.broadcasted_iota(jnp.int32, (LANES, LANES), 1)

    @pl.loop(0, rows // LANES)
    def _(k):
        part = pl.ds(pl.multiple_of(k * LANES, LANES), LANES)
        merged = None
        for a in reversed(range(4)):
            at = pl.ds(pl.multiple_of(a * rows + k * LANES, LANES), LANES)
            ends = jnp.where(lane < LANES // 2, picked[at, :], ship[at, :])
            turned = pltpu.roll(ends, 8 * a + EDGE, 1)
            merged = turned if merged is None else jnp.where(lane < 8 * a + 8, turned, merged)
        lines = merged.T[:4 * SUB, :]
        group = [lines[a * SUB:(a + 1) * SUB, :] for a in range(4)]
        for m in range(2):
            one, two = group[2 * m], group[2 * m + 1]
            pack_low[pl.ds(m * SUB, SUB), part] = jnp.where(upper, turn4(one), two)
            pack_high[pl.ds(m * SUB, SUB), part] = jnp.where(upper, one, turn4(two))
        pack_low[pl.ds(2 * SUB, SUB), part] = marks[1]
        pack_high[pl.ds(2 * SUB, SUB), part] = marks[1]

    pl.semaphore_wait(barrier, devices - 1)
    mid = pl.ds(LANES, rows)
    start, end = pl.ds(0, LANES), pl.ds(rows - LANES, LANES)
    above, under = pl.ds(0, LANES), pl.ds(rows + LANES, LANES)
    plan = [
        (near, got_bottom), (far, got_top), (pack_low, got_right.at[:, mid]), (pack_high, got_left.at[:, mid]),
        (pack_low.at[:, start], got_right.at[:, under]), (pack_high.at[:, start], got_left.at[:, under]),
        (pack_low.at[:, end], got_right.at[:, above]), (pack_high.at[:, end], got_left.at[:, above]),
    ]
    halos = []
    for k, (move, (src, dst)) in enumerate(zip(moves, plan)):
        inside, device = there(*move)
        copy = pltpu.make_async_remote_copy(src, dst, halo_send.at[k], halo_recv.at[k], device_id=device,
                                            device_id_type=MESH)
        pl.when(inside)(copy.start)
        halos.append((inside, there(-move[0], -move[1])[0], copy))

    @pl.loop(2, windows - 1)
    def _(s):
        for copy in loads(s, "middle"):
            copy.start()

    for copy in loads(0, "bottom") + loads(windows - 1, "top") + small[1:]:
        copy.start()

    lane8 = lax.broadcasted_iota(jnp.int32, (SUB, LANES), 1)
    at_last, at_first = lane8 == LANES - 1, lane8 == 0
    at_top = row8 == 0

    def rightward(vals):
        rolled = [pltpu.roll(v, LANES - 1, 1) for v in vals]
        return [jnp.where(at_last, rolled[(i + 1) % len(vals)], rolled[i]) for i in range(len(vals))]

    def leftward(vals):
        rolled = [pltpu.roll(v, 1, 1) for v in vals]
        return [jnp.where(at_first, rolled[i - 1], rolled[i]) for i in range(len(vals))]

    def scaled(v):
        return gravity * time_step * v, gravity * time_step * friction * v, time_step * v

    def factors(r):
        return [scaled(w[pl.ds(r, SUB), :])] * (n - 1) + [scaled(w8[pl.ds(r, SUB), :])]

    def update(eta, under_eta, tops, old_f, old_c, terms, carry, wanted):
        right = rightward(eta)
        cols = [face_update(old_c[i], eta[i], right[i], tops[1][i], *terms[i][:2]) for i in range(len(eta))]
        before = leftward(cols)
        carry, done = list(carry), {}
        for i in wanted:
            new = face_update(old_f[i], eta[i], under_eta[i], tops[0][i], *terms[i][:2])
            turned = pltpu.roll(new, 1, 0)
            up = jnp.where(at_top, carry[i], turned)
            carry[i] = turned
            done[i] = (eta[i] + terms[i][2] * (up - new + before[i] - cols[i]), new, cols[i])
        return done, carry

    def block(s, b, count, step, carry, slabs, state, tops, terms_of, wanted, store):
        m = len(slabs)
        at = [pl.multiple_of(s * win + (b + j) * SUB, SUB) for j in range(count)]
        zz = [pl.multiple_of((b + j) * SUB, SUB) for j in range(count)]
        own = state[0] is d
        wide_at = lambda i, j: slabs[i] * tall + at[j]
        here = wide_at if own else (lambda i, j: i * win + zz[j])
        source = (d, f, c) if step == 0 else state
        spot = wide_at if step == 0 else here
        pull = lambda ref, where, off=0: [[ref[pl.ds(where(i, j) + off, SUB), :] for i in range(m)] for j in range(count)]
        level, below = pull(source[0], spot), pull(source[0], spot, 1)
        old_f, old_c = pull(source[1], spot), pull(source[2], spot)
        if step == 0:
            bed, bed_below = pull(g, wide_at), pull(g, wide_at, 1)
        else:
            faces = [pull(ref, lambda i, j: i * win + zz[j]) for ref in tops]
        terms = [terms_of(r) for r in at]
        if step == STEPS - 1:
            floor = [{i: g[pl.ds(wide_at(i, j), SUB), :] for i in wanted} for j in range(count)]
        writes = []
        for j in range(count):
            eta, under_eta = level[j], below[j]
            if step == 0:
                eta = [x + y for x, y in zip(eta, bed[j])]
                under_eta = [x + y for x, y in zip(under_eta, bed_below[j])]
                face = ([jnp.maximum(x, y) for x, y in zip(bed[j], bed_below[j])],
                        [jnp.maximum(x, y) for x, y in zip(bed[j], rightward(bed[j]))])
                for ref, values in zip(tops, face):
                    for i in range(m):
                        writes.append((ref, i * win + zz[j], values[i]))
            else:
                face = (faces[0][j], faces[1][j])
            done, carry = update(eta, under_eta, face, old_f[j], old_c[j], terms[j], carry, wanted)
            for i, values in done.items():
                if step < STEPS - 1:
                    for ref, value in zip(state, values):
                        writes.append((ref, here(i, j), value))
                else:
                    done[i] = (values[0] - floor[j][i], values[1], values[2])
            if step == STEPS - 1:
                writes.append((None, j, done))
        for ref, where, value in writes:
            if ref is None:
                store(s, b + where, value)
            else:
                ref[pl.ds(where, SUB), :] = value
        return tuple(carry)

    def first_flow(s, slabs, state, top_rows, terms_of, wanted):
        r = pl.multiple_of(s * win, SUB)
        terms = terms_of(r)
        carry = []
        for i in range(len(slabs)):
            if i not in wanted:
                carry.append(blank)
                continue
            at = slabs[i] * tall + r if state[0] is d else i * win
            eta, under_eta, old = (ref[pl.ds(at + off, SUB), :] for ref, off in ((state[0], 0), (state[0], 1), (state[1], 0)))
            new = face_update(old, eta, under_eta, top_rows[pl.ds(i * win, SUB), :], *terms[i][:2])
            carry.append(pltpu.roll(new, 1, 0))
        return tuple(carry)

    def window(s, slabs, state, tops, terms_of, wanted, store, group, last_group):
        every = tuple(range(len(slabs)))
        for step in range(STEPS - 1):
            lax.fori_loop(0, (SEG + 16) // SUB // group, lambda k, old, step=step: block(
                s, k * group, group, step, old, slabs, state, tops, terms_of, every, store), (blank,) * len(slabs))
        lax.fori_loop(0, SEG // SUB // last_group, lambda k, old: block(
            s, k * last_group + 1, last_group, STEPS - 1, old, slabs, state, tops, terms_of, wanted, store),
            first_flow(s, slabs, state, tops[0], terms_of, wanted))

    gives_right, gives_down = me_col < n_col - 1, me_row < n_row - 1
    takes_left, takes_up = me_col > 0, me_row > 0
    own_terms = [scaled(wet_value)] * 3

    def store_early(s, b, done):
        at = pl.multiple_of(b * SUB - SUB, SUB)
        for a, value in enumerate(done[1]):
            early[s - 1, a, pl.ds(at, SUB), :] = value

    def early_copies(s):
        at = pl.multiple_of((windows - 1 - s) * SEG, SEG)
        return [pltpu.make_async_remote_copy(
            early.at[s - 1, a], moved_cols.at[a, pl.ds(at, SEG)],
            early_send.at[a, s], early_recv.at[a, s], device_id=(me_row, me_col + 1), device_id_type=MESH)
            for a in range(3)]

    @pl.loop(1, 1 + EARLY)
    def _(s):
        for copy in loads(s, "middle"):
            copy.wait()
        window(s, [near_right - 1, near_right, near_right + 1], (early_d, early_f, early_c), (early_zr, early_zc),
               lambda r: own_terms, (1,), store_early, EARLY_GROUP, EARLY_LAST)

        @pl.when(jnp.logical_and(gives_right, s < 1 + EARLY_NOW))
        def _():
            for copy in early_copies(s):
                copy.start()

    w[...] = jnp.concatenate([wet_value] * (tall // SUB), axis=0)
    for copy in small[1:]:
        copy.wait()
    cell = cell_v[...]
    cell_row, cell_col = cell // width, cell % width
    turn = cell_row // SEG
    spot_v[...] = cell_col // LANES * tall + (windows - 1 - turn) * win + SUB + cell_row - turn * SEG
    to_scalar = [pltpu.make_async_copy(spot_v.at[k], spot_s.at[pl.ds(k * LANES, LANES)], spot_sem.at[k])
                 for k in range(spot_v.shape[0])]
    for copy in to_scalar:
        copy.start()

    for sent, fed, copy in halos:
        pl.when(sent)(copy.wait_send)
        pl.when(fed)(copy.wait_recv)

    @pl.loop(1 + EARLY_NOW, 1 + EARLY)
    def _(s):
        @pl.when(gives_right)
        def _():
            for copy in early_copies(s):
                copy.start()

    rest = jnp.zeros((LANES - 5 * SUB, LANES), jnp.float32)

    @pl.loop(0, rows // LANES + 2)
    def _(k):
        part = pl.ds(pl.multiple_of(k * LANES, LANES), LANES)
        both = []
        for m in range(3):
            left, right = (ref[pl.ds(m * SUB, SUB), part] for ref in (got_left, got_right))
            both.append(jnp.where(upper, left, turn4(right)))
            both.append(jnp.where(upper, turn4(left), right))
        side[part, :] = jnp.concatenate(both[:5] + [rest], axis=0).T

    @pl.loop(0, windows)
    def _(s):
        mixed = side[pl.ds(pl.multiple_of((windows - 1 - s) * SEG + LANES - SUB, SUB), SEG + 16), :]
        at = pl.multiple_of(s * win, SUB)
        for a, dst in enumerate((d, g, f, c, w8)):
            base = (n - 1) * tall if a < 4 else 0
            dst[pl.ds(base + at, SEG + 16), :] = pltpu.roll(mixed, LANES - 8 * a - EDGE, 1)

    for a, (_, dst) in enumerate(arrays):
        for i in range(n - 1):
            lanes = pl.ds(i * LANES, LANES)
            top, under = (ref[pl.ds(a // 2 * SUB, SUB), lanes] for ref in (got_top, got_bottom))
            dst[pl.ds(i * tall + (windows - 1) * win, SUB), :] = top if a % 2 else turn4(top)
            dst[pl.ds(i * tall + SEG + SUB, SUB), :] = turn4(under) if a % 2 else under
    w[pl.ds((windows - 1) * win, SUB), :] = turn4(got_top[pl.ds(2 * SUB, SUB), pl.ds(0, LANES)])
    w[pl.ds(SEG + SUB, SUB), :] = got_bottom[pl.ds(2 * SUB, SUB), pl.ds(0, LANES)]

    def store_main(s, b, done):
        at = pl.multiple_of((windows - 1 - s) * SEG + b * SUB - SUB, SUB)
        for i, values in done.items():
            d[pl.ds(pl.multiple_of(i * tall + s * win + b * SUB, SUB), SUB), :] = values[0]
            for a, value in enumerate(values):
                fin[a, pl.ds(at, SUB), pl.ds(i * LANES, LANES)] = value
                if i >= near_right:
                    ship[pl.ds(pl.multiple_of(((i - near_right) * 3 + a) * rows + at, SUB), SUB), :] = value

    def out_copies(s):
        at = pl.multiple_of((windows - 1 - s) * SEG, SEG)
        return [pltpu.make_async_copy(fin.at[a, pl.ds(at, SEG), :], ref.at[pl.ds(at, SEG), :], out_sem.at[a, s])
                for a, ref in enumerate((out_d, out_f, out_c))]

    def col_copies(s, k):
        at = pl.multiple_of((windows - 1 - s) * SEG, SEG)
        return [pltpu.make_async_remote_copy(
            ship.at[pl.ds(pl.multiple_of((k * 3 + a) * rows + at, SEG), SEG)], moved_cols.at[k * 3 + a, pl.ds(at, SEG)],
            col_send.at[k * 3 + a, s], col_recv.at[k * 3 + a, s], device_id=(me_row, me_col + 1), device_id_type=MESH)
            for a in range(3)]

    def row_copies(s):
        at = pl.multiple_of((windows - 1 - s) * SEG, SEG)
        to = pl.multiple_of(span - SEG - s * SEG, SEG)
        return [pltpu.make_async_remote_copy(
            fin.at[a, pl.ds(at, SEG), :], moved_rows.at[a, pl.ds(to, SEG), :],
            row_send.at[a, s], row_recv.at[a, s], device_id=(me_row + 1, me_col), device_id_type=MESH)
            for a in range(3)]

    def outer(s):
        return jnp.logical_or(s == 0, s > EARLY)

    @pl.loop(0, windows)
    def _(s):
        for kind, index in (("bottom", 0), ("top", windows - 1)):
            @pl.when(s == index)
            def _():
                for copy in loads(index, kind):
                    copy.wait()

        @pl.when(jnp.logical_and(s > EARLY, s < windows - 1))
        def _():
            for copy in loads(s, "middle"):
                copy.wait()

        window(s, list(range(n)), (d, f, c), (zr, zc), factors, tuple(range(n - 1)), store_main, GROUP, LAST)
        for k, holds in ((0, outer(s)), (1, True)):
            @pl.when(jnp.logical_and(jnp.logical_and(gives_right, s < windows - HELD), holds))
            def _():
                for copy in col_copies(s, k):
                    copy.start()

        @pl.when(jnp.logical_and(gives_down, s < span // SEG))
        def _():
            for copy in row_copies(s):
                copy.start()

        for copy in out_copies(s):
            copy.start()

    for copy in to_scalar:
        copy.wait()

    @pl.loop(0, picked.shape[0] // 16)
    def _(k):
        base = pl.multiple_of(k * 16, 16)
        rows16 = [d[pl.ds(spot_s[base + j], 1), :] for j in range(16)]
        for j in range(16):
            picked[pl.ds(base + j, 1), :] = rows16[j]

    acc[...] = jnp.zeros_like(acc)
    deep = lax.broadcasted_iota(jnp.int32, (LANES, LANES), 0)
    wide = lax.broadcasted_iota(jnp.int32, (devices, LANES), 0)

    @pl.loop(0, picked.shape[0] // LANES // LINES)
    def _(k):
        total = acc[...]
        for j in range(LINES):
            line = pl.ds(k * LINES + j, 1)
            chunk = picked[pl.ds(pl.multiple_of((k * LINES + j) * LANES, LANES), LANES), :].T
            chosen = jnp.sum(jnp.where(deep == cell_v[line, :] % LANES, chunk, 0.0), axis=0, keepdims=True)
            captured = coef_v[line, :] * jnp.maximum(chosen, 0.0)
            node = node_v[line, :]
            mine = wide == node // NODE_DEV
            pieces = []
            for _ in range(3):
                piece = captured.astype(jnp.bfloat16).astype(jnp.float32)
                pieces.append(jnp.where(mine, piece, 0.0).astype(jnp.bfloat16))
                captured = captured - piece
            within = (deep == node % NODE_DEV).astype(jnp.bfloat16)
            total = total + lax.dot_general(jnp.concatenate(pieces, axis=0), within, (((1,), (1,)), ((), ())),
                                            preferred_element_type=jnp.float32)
        acc[...] = total

    for k in range(devices):
        parts[k] = acc[pl.ds(k, 1), :] + acc[pl.ds(devices + k, 1), :] + acc[pl.ds(2 * devices + k, 1), :]

    def send(k):
        other, device = place(k)
        return pltpu.make_async_remote_copy(parts.at[other], slots.at[k], node_send.at[k], node_recv.at[k],
                                            device_id=device, device_id_type=MESH)

    @pl.loop(1, devices)
    def _(k):
        send(k).start()

    for s in range(windows - HELD, windows):
        @pl.when(gives_right)
        def _():
            for copy in col_copies(s, 0) + col_copies(s, 1):
                copy.start()

    @pl.loop(1, devices)
    def _(k):
        send(k).wait()

    note[pl.ds(0, 1), :] = parts[me] + jnp.sum(slots[pl.ds(1, devices - 1)], axis=0)
    note[pl.ds(1, 1), :] = got_top[pl.ds(2 * SUB + EDGE, 1), pl.ds(0, LANES)]
    note[pl.ds(2, 1), :] = got_left[pl.ds(2 * SUB + EDGE, 1), pl.ds(LANES, LANES)]
    note[pl.ds(3, 5), :] = jnp.zeros((5, LANES), jnp.float32)
    last = pltpu.make_async_copy(note, extra, small_sem.at[5])
    last.start()

    @pl.loop(0, windows)
    def _(s):
        for copy in out_copies(s):
            copy.wait()
        for some, holds in ((col_copies(s, 0), outer(s)), (col_copies(s, 1), True),
                            (early_copies(s), jnp.logical_not(outer(s)))):
            for copy in some:
                pl.when(jnp.logical_and(gives_right, holds))(copy.wait_send)
                pl.when(jnp.logical_and(takes_left, holds))(copy.wait_recv)
        for copy in row_copies(s):
            pl.when(jnp.logical_and(gives_down, s < span // SEG))(copy.wait_send)
            pl.when(jnp.logical_and(takes_up, s < span // SEG))(copy.wait_recv)

    last.wait()


def fused(arrays, flags, cells, nodes, coefs):
    rows, width = arrays[0].shape
    counts = (lax.axis_size("row"), lax.axis_size("col"))
    devices = counts[0] * counts[1]
    span = MAX_BLOCKS * BLOCK
    n, windows, win = width // LANES + 1, rows // SEG, SEG + 24
    tall = windows * win
    lines = cells.shape[0]
    hbm, free = pl.BlockSpec(memory_space=pltpu.HBM), pl.BlockSpec(memory_space=pl.ANY)
    vmem = lambda *shape: pltpu.VMEM(shape, jnp.float32)
    sems = lambda *shape: pltpu.SemaphoreType.DMA(shape)
    across, along = (3 * SUB, width), (3 * SUB, rows + 2 * LANES)
    raw, part = (4 * SUB, width), (3 * win, LANES)
    shapes = [(rows, width)] * 3 + [(3, span, width), (3 * MAX_BLOCKS, rows, LANES), (SUB, LANES)]
    state = vmem(n * tall, LANES)
    return pl.pallas_call(
        functools.partial(fused_kernel, counts),
        out_shape=[jax.ShapeDtypeStruct(shape, jnp.float32) for shape in shapes],
        in_specs=[hbm] * 4 + [free] + [hbm] * 3,
        out_specs=[free] * len(shapes),
        scratch_shapes=[
            state, state, state, state, vmem(tall, LANES), vmem(tall, LANES), vmem(n * win, LANES), vmem(n * win, LANES),
            vmem(3, rows, width), vmem(*part), vmem(*part), vmem(*part), vmem(*part), vmem(*part),
            vmem(EARLY, 3, SEG, LANES), vmem(3 * MAX_BLOCKS * rows, LANES), vmem(3 * SUB, rows),
            vmem(3 * SUB, rows), vmem(*raw), vmem(*raw), vmem(*across), vmem(*across), vmem(*across), vmem(*across),
            vmem(*along), vmem(*along), vmem(rows + 2 * LANES, LANES), vmem(SUB, LANES),
            pltpu.VMEM((lines, LANES), jnp.int32), pltpu.VMEM((lines, LANES), jnp.int32), vmem(lines, LANES),
            pltpu.VMEM((lines, LANES), jnp.int32), vmem(lines * LANES, LANES), vmem(3 * devices, LANES),
            vmem(devices, 1, LANES), vmem(devices, 1, LANES), vmem(SUB, LANES), pltpu.SMEM((lines * LANES,), jnp.int32),
            sems(windows, 4, n), sems(4, 4), sems(8), sems(8), sems(8), sems(3, windows), sems(6, windows),
            sems(6, windows), sems(3, windows), sems(3, windows), sems(3, windows), sems(3, windows), sems(devices),
            sems(devices), sems(lines),
        ],
        compiler_params=pltpu.CompilerParams(collective_id=0, has_side_effects=True, vmem_limit_bytes=38 << 20),
        name="fused",
    )(*arrays, flags, *[pltpu.with_memory_space_constraint(x, pltpu.HBM) for x in (cells, nodes, coefs)])


def finish_kernel(d, f, c, rows_in, cols_in, extra, out_d, out_f, out_c, out_rows, out_cols, out_node,
                  zero_rows, zero_cols, note, sem, row_sem, col_sem, note_sem):
    fetch = pltpu.make_async_copy(extra, note, note_sem.at[0])
    fetch.start()
    copies = [pltpu.make_async_copy(src, dst, sem.at[a]) for a, (src, dst) in enumerate(
        ((d, out_d), (f, out_f), (c, out_c)))]
    for copy in copies:
        copy.start()
    zero_rows[...] = jnp.zeros_like(zero_rows)
    zero_cols[...] = jnp.zeros_like(zero_cols)
    fetch.wait()
    given_rows = jnp.max(note[pl.ds(1, 1), :])
    given_cols = jnp.max(note[pl.ds(2, 1), :])

    def hand_on(src, hole, dst, one, keep):
        copy = pltpu.make_async_copy(src, dst, one)
        fill = pltpu.make_async_copy(hole, dst, one)
        pl.when(keep)(copy.start)
        pl.when(jnp.logical_not(keep))(fill.start)
        copies.append(copy)

    for k in range(MAX_BLOCKS):
        part = pl.ds(k * BLOCK, BLOCK)
        for a in range(3):
            hand_on(rows_in.at[a, part, :], zero_rows, out_rows.at[a, part, :], row_sem.at[a, k],
                    given_rows >= MAX_BLOCKS - k)
            hand_on(cols_in.at[k * 3 + a], zero_cols, out_cols.at[a, :, part], col_sem.at[a, k],
                    given_cols >= MAX_BLOCKS - k)
    out_node[...] = note[pl.ds(0, 1), pl.ds(0, NODE_DEV)]
    for copy in copies:
        copy.wait()


def finish(d, f, c, moved_rows, moved_cols, extra):
    rows, width = d.shape
    free, hbm = pl.BlockSpec(memory_space=pl.ANY), pl.BlockSpec(memory_space=pltpu.HBM)
    shapes = [x.shape for x in (d, f, c, moved_rows)] + [(3, rows, MAX_BLOCKS * BLOCK), (1, NODE_DEV)]
    return pl.pallas_call(
        finish_kernel,
        out_shape=[jax.ShapeDtypeStruct(shape, jnp.float32) for shape in shapes],
        in_specs=[free] * 6,
        out_specs=[hbm] * 5 + [pl.BlockSpec(memory_space=pltpu.VMEM)],
        scratch_shapes=[pltpu.VMEM((BLOCK, width), jnp.float32), pltpu.VMEM((rows, BLOCK), jnp.float32),
                        pltpu.VMEM((SUB, LANES), jnp.float32), pltpu.SemaphoreType.DMA((3,)),
                        pltpu.SemaphoreType.DMA((3, MAX_BLOCKS)), pltpu.SemaphoreType.DMA((3, MAX_BLOCKS)),
                        pltpu.SemaphoreType.DMA((1,))],
        compiler_params=pltpu.CompilerParams(vmem_limit_bytes=2 << 20),
        name="finish",
    )(d, f, c, moved_rows, moved_cols, extra)


def body(
    depth,
    ground,
    flow_rows,
    flow_cols,
    wet_tiles,
    inlet_cell,
    inlet_node,
    inlet_coef,
    shift_rows,
    shift_cols,
):
    flat = lambda x: x.reshape(-1, LANES)
    flags = sum(jnp.pad(value, ((k, SUB - 1 - k), (0, LANES - 1)))
                for k, value in enumerate((wet_tiles, shift_rows, shift_cols))).astype(jnp.float32)
    results = fused((depth, ground, flow_rows, flow_cols), flags,
                    flat(inlet_cell), flat(inlet_node), flat(inlet_coef))
    depth, flow_rows, flow_cols, moved_rows, moved_cols, node_inflow = finish(*results)
    return (depth, flow_rows, flow_cols, node_inflow[0], moved_rows, moved_cols)


def solution(mesh):
    return jax.shard_map(
        body,
        mesh=mesh,
        in_specs=(
            P("row", "col"),
            P("row", "col"),
            P("row", "col"),
            P("row", "col"),
            P("row", "col"),
            P("row", "col", None),
            P("row", "col", None),
            P("row", "col", None),
            P("row", "col"),
            P("row", "col"),
        ),
        out_specs=(
            P("row", "col"),
            P("row", "col"),
            P("row", "col"),
            P(("row", "col")),
            P(None, "row", "col"),
            P(None, "row", "col"),
        ),
        check_vma=False,
    )
```

```python
import functools

import jax
import jax.numpy as jnp
from jax import lax
from jax.experimental import pallas as pl
from jax.experimental.pallas import tpu as pltpu
from jax.sharding import PartitionSpec as P

STEPS = 3
BLOCK = 128
MAX_BLOCKS = 2
NODE_DEV = 64
LANES = 128
SUB = 8
EDGE = 4
GROUP = 3
EARLY_GROUP = 6
EARLY_LAST = 4
EARLY = 2
LAST = 4
HELD = 1
SHARES = 4
LINES = 4
SEG = 128
MESH = pl.DeviceIdType.MESH


gravity = 9.81
time_step = 0.1
friction = 0.0025
depth_floor = 0.25
POWER = -7.0 / 3.0


def face_update(flow, eta, eta_next, top, pull, rub):
    over = jnp.maximum(eta, eta_next) - top
    root = jnp.exp2(POWER * lax.log2(jnp.maximum(over, depth_floor)))
    drag = rub * jnp.abs(flow) * root
    pushed = flow - pull * jnp.maximum(over, 0.0) * (eta_next - eta)
    return pushed * pl.reciprocal(1.0 + drag)


def fused_kernel(counts, *refs):
    depth, ground, frow, fcol, flags, cells, nodes, coefs = refs[:8]
    out_d, out_f, out_c, moved_rows, moved_cols, extra = refs[8:14]
    (d, g, f, c, w, w8, zr, zc, fin, early_d, early_f, early_c, early_zr, early_zc, early, ship,
     pack_low, pack_high, first_rows, last_rows, near, far, got_top, got_bottom, got_left, got_right, side,
     flag_v, cell_v, node_v, coef_v, spot_v, picked, acc, parts, slots, note, spot_s,
     in_sem, edge_sem, small_sem, halo_send, halo_recv, out_sem, col_send, col_recv, row_send, row_recv,
     early_send, early_recv, node_send, node_recv, spot_sem) = refs[14:]
    n_row, n_col = counts
    devices = n_row * n_col
    rows, width = depth.shape
    n = width // LANES + 1
    windows = rows // SEG
    win = SEG + 24
    tall = windows * win
    span = MAX_BLOCKS * BLOCK
    near_right = (width - span) // LANES
    me_row, me_col = lax.axis_index("row"), lax.axis_index("col")
    me = me_row * n_col + me_col
    moves = [(-1, 0), (1, 0), (0, -1), (0, 1), (-1, -1), (-1, 1), (1, -1), (1, 1)]
    arrays = ((depth, d), (ground, g), (frow, f), (fcol, c))

    def place(k):
        other = lax.rem(me + k, devices)
        return other, (other // n_col, lax.rem(other, n_col))

    def there(dr, dc):
        r, q = me_row + dr, me_col + dc
        inside = jnp.logical_and(jnp.logical_and(r >= 0, r < n_row), jnp.logical_and(q >= 0, q < n_col))
        return inside, (r, q)

    small = [pltpu.make_async_copy(src, dst, small_sem.at[k]) for k, (src, dst) in enumerate((
        (flags, flag_v), (cells, cell_v), (nodes, node_v), (coefs, coef_v)))]
    small[0].start()
    edges = []
    for a, (src, _) in enumerate(arrays):
        for k, (piece, dst) in enumerate((
            (src.at[:, pl.ds(0, LANES)], picked.at[pl.ds(a * rows, rows)]),
            (src.at[:, pl.ds(width - LANES, LANES)], ship.at[pl.ds(a * rows, rows)]),
            (src.at[pl.ds(0, SUB), :], first_rows.at[pl.ds(a * SUB, SUB), :]),
            (src.at[pl.ds(rows - SUB, SUB), :], last_rows.at[pl.ds(a * SUB, SUB), :]),
        )):
            edges.append(pltpu.make_async_copy(piece, dst, edge_sem.at[a, k]))
            edges[-1].start()

    for ref in (got_top, got_bottom, got_left, got_right):
        ref[...] = jnp.zeros_like(ref)
    barrier = pltpu.get_barrier_semaphore()

    @pl.loop(1, devices)
    def _(k):
        pl.semaphore_signal(barrier, inc=1, device_id=place(k)[1], device_id_type=MESH)

    def loads(s, kind):
        lead, trail = (0 if kind == "top" else SUB), (0 if kind == "bottom" else SUB)
        start = (windows - 1 - s) * SEG - lead
        at = s * win + SUB - lead
        if not isinstance(s, int):
            start, at = pl.multiple_of(start, SUB), pl.multiple_of(at, SUB)
        high_rows = SEG + lead + trail
        return [pltpu.make_async_copy(src.at[pl.ds(start, high_rows), pl.ds(i * LANES, LANES)],
                                      dst.at[pl.ds(i * tall + at, high_rows)], in_sem.at[s, a, i])
                for a, (src, dst) in enumerate(arrays) for i in range(n - 1)]

    for copy in loads(1, "middle"):
        copy.start()

    blank = jnp.zeros((SUB, LANES), jnp.float32)
    for buf in (d, g):
        for i in range(n):
            for s in range(windows):
                buf[pl.ds(i * tall + s * win + SEG + 16, SUB), :] = blank
    for i in range(3):
        early_d[pl.ds(i * win + SEG + 16, SUB), :] = blank
    small[0].wait()
    flag = lambda k: jnp.broadcast_to(jnp.broadcast_to(flag_v[pl.ds(k, 1), :][:, :1], (1, LANES)), (SUB, LANES))
    wet_value = flag(0)
    row8 = lax.broadcasted_iota(jnp.int32, (SUB, LANES), 0)
    upper = row8 < EDGE
    marks = [jnp.where(upper, wet_value, flag(k)) for k in (1, 2)]
    turn4 = lambda v: pltpu.roll(v, EDGE, 0)
    for copy in edges:
        copy.wait()
    for i in range(n - 1):
        lanes = pl.ds(i * LANES, LANES)
        for m in range(2):
            part = pl.ds(m * SUB, SUB)
            one, two = pl.ds(2 * m * SUB, SUB), pl.ds((2 * m + 1) * SUB, SUB)
            near[part, lanes] = jnp.where(upper, first_rows[one, lanes], turn4(first_rows[two, lanes]))
            far[part, lanes] = jnp.where(upper, turn4(last_rows[one, lanes]), last_rows[two, lanes])
        near[pl.ds(2 * SUB, SUB), lanes] = marks[0]
        far[pl.ds(2 * SUB, SUB), lanes] = marks[0]
    lane = lax.broadcasted_iota(jnp.int32, (LANES, LANES), 1)

    @pl.loop(0, rows // LANES)
    def _(k):
        part = pl.ds(pl.multiple_of(k * LANES, LANES), LANES)
        merged = None
        for a in reversed(range(4)):
            at = pl.ds(pl.multiple_of(a * rows + k * LANES, LANES), LANES)
            ends = jnp.where(lane < LANES // 2, picked[at, :], ship[at, :])
            turned = pltpu.roll(ends, 8 * a + EDGE, 1)
            merged = turned if merged is None else jnp.where(lane < 8 * a + 8, turned, merged)
        lines = merged.T[:4 * SUB, :]
        group = [lines[a * SUB:(a + 1) * SUB, :] for a in range(4)]
        for m in range(2):
            one, two = group[2 * m], group[2 * m + 1]
            pack_low[pl.ds(m * SUB, SUB), part] = jnp.where(upper, turn4(one), two)
            pack_high[pl.ds(m * SUB, SUB), part] = jnp.where(upper, one, turn4(two))
        pack_low[pl.ds(2 * SUB, SUB), part] = marks[1]
        pack_high[pl.ds(2 * SUB, SUB), part] = marks[1]

    pl.semaphore_wait(barrier, devices - 1)
    mid = pl.ds(LANES, rows)
    start, end = pl.ds(0, LANES), pl.ds(rows - LANES, LANES)
    above, under = pl.ds(0, LANES), pl.ds(rows + LANES, LANES)
    plan = [
        (near, got_bottom), (far, got_top), (pack_low, got_right.at[:, mid]), (pack_high, got_left.at[:, mid]),
        (pack_low.at[:, start], got_right.at[:, under]), (pack_high.at[:, start], got_left.at[:, under]),
        (pack_low.at[:, end], got_right.at[:, above]), (pack_high.at[:, end], got_left.at[:, above]),
    ]
    halos = []
    for k, (move, (src, dst)) in enumerate(zip(moves, plan)):
        inside, device = there(*move)
        copy = pltpu.make_async_remote_copy(src, dst, halo_send.at[k], halo_recv.at[k], device_id=device,
                                            device_id_type=MESH)
        pl.when(inside)(copy.start)
        halos.append((inside, there(-move[0], -move[1])[0], copy))

    @pl.loop(2, 1 + EARLY)
    def _(s):
        for copy in loads(s, "middle"):
            copy.start()

    for copy in small[1:]:
        copy.start()

    lane8 = lax.broadcasted_iota(jnp.int32, (SUB, LANES), 1)
    at_last, at_first = lane8 == LANES - 1, lane8 == 0
    at_top = row8 == 0

    def rightward(vals):
        rolled = [pltpu.roll(v, LANES - 1, 1) for v in vals]
        return [jnp.where(at_last, rolled[(i + 1) % len(vals)], rolled[i]) for i in range(len(vals))]

    def leftward(vals):
        rolled = [pltpu.roll(v, 1, 1) for v in vals]
        return [jnp.where(at_first, rolled[i - 1], rolled[i]) for i in range(len(vals))]

    def scaled(v):
        return gravity * time_step * v, gravity * time_step * friction * v, time_step * v

    def factors(r):
        return [scaled(w[pl.ds(r, SUB), :])] * (n - 1) + [scaled(w8[pl.ds(r, SUB), :])]

    def update(eta, under_eta, tops, old_f, old_c, terms, carry, wanted):
        right = rightward(eta)
        cols = [face_update(old_c[i], eta[i], right[i], tops[1][i], *terms[i][:2]) for i in range(len(eta))]
        before = leftward(cols)
        carry, done = list(carry), {}
        for i in wanted:
            new = face_update(old_f[i], eta[i], under_eta[i], tops[0][i], *terms[i][:2])
            turned = pltpu.roll(new, 1, 0)
            up = jnp.where(at_top, carry[i], turned)
            carry[i] = turned
            done[i] = (eta[i] + terms[i][2] * (up - new + before[i] - cols[i]), new, cols[i])
        return done, carry

    def block(s, b, count, step, carry, slabs, state, tops, terms_of, wanted, store):
        m = len(slabs)
        at = [pl.multiple_of(s * win + (b + j) * SUB, SUB) for j in range(count)]
        zz = [pl.multiple_of((b + j) * SUB, SUB) for j in range(count)]
        own = state[0] is d
        wide_at = lambda i, j: slabs[i] * tall + at[j]
        here = wide_at if own else (lambda i, j: i * win + zz[j])
        source = (d, f, c) if step == 0 else state
        spot = wide_at if step == 0 else here
        pull = lambda ref, where, off=0: [[ref[pl.ds(where(i, j) + off, SUB), :] for i in range(m)] for j in range(count)]
        level, below = pull(source[0], spot), pull(source[0], spot, 1)
        old_f, old_c = pull(source[1], spot), pull(source[2], spot)
        if step == 0:
            bed, bed_below = pull(g, wide_at), pull(g, wide_at, 1)
        else:
            faces = [pull(ref, lambda i, j: i * win + zz[j]) for ref in tops]
        terms = [terms_of(r) for r in at]
        if step == STEPS - 1:
            floor = [{i: g[pl.ds(wide_at(i, j), SUB), :] for i in wanted} for j in range(count)]
        writes = []
        for j in range(count):
            eta, under_eta = level[j], below[j]
            if step == 0:
                eta = [x + y for x, y in zip(eta, bed[j])]
                under_eta = [x + y for x, y in zip(under_eta, bed_below[j])]
                face = ([jnp.maximum(x, y) for x, y in zip(bed[j], bed_below[j])],
                        [jnp.maximum(x, y) for x, y in zip(bed[j], rightward(bed[j]))])
                for ref, values in zip(tops, face):
                    for i in range(m):
                        writes.append((ref, i * win + zz[j], values[i]))
            else:
                face = (faces[0][j], faces[1][j])
            done, carry = update(eta, under_eta, face, old_f[j], old_c[j], terms[j], carry, wanted)
            for i, values in done.items():
                if step < STEPS - 1:
                    for ref, value in zip(state, values):
                        writes.append((ref, here(i, j), value))
                else:
                    done[i] = (values[0] - floor[j][i], values[1], values[2])
            if step == STEPS - 1:
                writes.append((None, j, done))
        for ref, where, value in writes:
            if ref is None:
                store(s, b + where, value)
            else:
                ref[pl.ds(where, SUB), :] = value
        return tuple(carry)

    def first_flow(s, slabs, state, top_rows, terms_of, wanted):
        r = pl.multiple_of(s * win, SUB)
        terms = terms_of(r)
        carry = []
        for i in range(len(slabs)):
            if i not in wanted:
                carry.append(blank)
                continue
            at = slabs[i] * tall + r if state[0] is d else i * win
            eta, under_eta, old = (ref[pl.ds(at + off, SUB), :] for ref, off in ((state[0], 0), (state[0], 1), (state[1], 0)))
            new = face_update(old, eta, under_eta, top_rows[pl.ds(i * win, SUB), :], *terms[i][:2])
            carry.append(pltpu.roll(new, 1, 0))
        return tuple(carry)

    def window(s, slabs, state, tops, terms_of, wanted, store, group, last_group):
        every = tuple(range(len(slabs)))
        for step in range(STEPS - 1):
            lax.fori_loop(0, (SEG + 16) // SUB // group, lambda k, old, step=step: block(
                s, k * group, group, step, old, slabs, state, tops, terms_of, every, store), (blank,) * len(slabs))
        lax.fori_loop(0, SEG // SUB // last_group, lambda k, old: block(
            s, k * last_group + 1, last_group, STEPS - 1, old, slabs, state, tops, terms_of, wanted, store),
            first_flow(s, slabs, state, tops[0], terms_of, wanted))

    gives_right, gives_down = me_col < n_col - 1, me_row < n_row - 1
    takes_left, takes_up = me_col > 0, me_row > 0
    own_terms = [scaled(wet_value)] * 3

    def store_early(s, b, done):
        at = pl.multiple_of(b * SUB - SUB, SUB)
        for a, value in enumerate(done[1]):
            early[s - 1, a, pl.ds(at, SUB), :] = value

    def early_copies(s):
        at = pl.multiple_of((windows - 1 - s) * SEG, SEG)
        return [pltpu.make_async_remote_copy(
            early.at[s - 1, a], moved_cols.at[a, pl.ds(at, SEG)],
            early_send.at[a, s], early_recv.at[a, s], device_id=(me_row, me_col + 1), device_id_type=MESH)
            for a in range(3)]

    @pl.loop(1, 1 + EARLY)
    def _(s):
        for copy in loads(s, "middle"):
            copy.wait()
        window(s, [near_right - 1, near_right, near_right + 1], (early_d, early_f, early_c), (early_zr, early_zc),
               lambda r: own_terms, (1,), store_early, EARLY_GROUP, EARLY_LAST)

        @pl.when(s == 1)
        def _():
            for sent, fed, copy in halos:
                pl.when(sent)(copy.wait_send)
                pl.when(fed)(copy.wait_recv)

        @pl.when(gives_right)
        def _():
            for copy in early_copies(s):
                copy.start()

    for copy in loads(0, "bottom"):
        copy.start()

    @pl.loop(1 + EARLY, windows - 1)
    def _(s):
        for copy in loads(s, "middle"):
            copy.start()

    for copy in loads(windows - 1, "top"):
        copy.start()
    w[...] = jnp.concatenate([wet_value] * (tall // SUB), axis=0)
    for copy in small[1:]:
        copy.wait()
    cell = cell_v[...]
    cell_row, cell_col = cell // width, cell % width
    turn = cell_row // SEG
    spot_v[...] = cell_col // LANES * tall + (windows - 1 - turn) * win + SUB + cell_row - turn * SEG
    to_scalar = [pltpu.make_async_copy(spot_v.at[k], spot_s.at[pl.ds(k * LANES, LANES)], spot_sem.at[k])
                 for k in range(spot_v.shape[0])]
    for copy in to_scalar:
        copy.start()

    rest = jnp.zeros((LANES - 5 * SUB, LANES), jnp.float32)

    @pl.loop(0, rows // LANES + 2)
    def _(k):
        part = pl.ds(pl.multiple_of(k * LANES, LANES), LANES)
        both = []
        for m in range(3):
            left, right = (ref[pl.ds(m * SUB, SUB), part] for ref in (got_left, got_right))
            both.append(jnp.where(upper, left, turn4(right)))
            both.append(jnp.where(upper, turn4(left), right))
        side[part, :] = jnp.concatenate(both[:5] + [rest], axis=0).T

    @pl.loop(0, windows)
    def _(s):
        mixed = side[pl.ds(pl.multiple_of((windows - 1 - s) * SEG + LANES - SUB, SUB), SEG + 16), :]
        at = pl.multiple_of(s * win, SUB)
        for a, dst in enumerate((d, g, f, c, w8)):
            base = (n - 1) * tall if a < 4 else 0
            dst[pl.ds(base + at, SEG + 16), :] = pltpu.roll(mixed, LANES - 8 * a - EDGE, 1)

    for a, (_, dst) in enumerate(arrays):
        for i in range(n - 1):
            lanes = pl.ds(i * LANES, LANES)
            top, under = (ref[pl.ds(a // 2 * SUB, SUB), lanes] for ref in (got_top, got_bottom))
            dst[pl.ds(i * tall + (windows - 1) * win, SUB), :] = top if a % 2 else turn4(top)
            dst[pl.ds(i * tall + SEG + SUB, SUB), :] = turn4(under) if a % 2 else under
    w[pl.ds((windows - 1) * win, SUB), :] = turn4(got_top[pl.ds(2 * SUB, SUB), pl.ds(0, LANES)])
    w[pl.ds(SEG + SUB, SUB), :] = got_bottom[pl.ds(2 * SUB, SUB), pl.ds(0, LANES)]

    def store_main(s, b, done):
        at = pl.multiple_of((windows - 1 - s) * SEG + b * SUB - SUB, SUB)
        for i, values in done.items():
            d[pl.ds(pl.multiple_of(i * tall + s * win + b * SUB, SUB), SUB), :] = values[0]
            for a, value in enumerate(values):
                fin[a, pl.ds(at, SUB), pl.ds(i * LANES, LANES)] = value
                if i >= near_right:
                    ship[pl.ds(pl.multiple_of(((i - near_right) * 3 + a) * rows + at, SUB), SUB), :] = value

    def out_copies(s):
        at = pl.multiple_of((windows - 1 - s) * SEG, SEG)
        return [pltpu.make_async_copy(fin.at[a, pl.ds(at, SEG), :], ref.at[pl.ds(at, SEG), :], out_sem.at[a, s])
                for a, ref in enumerate((out_d, out_f, out_c))]

    def col_copies(s, k):
        at = pl.multiple_of((windows - 1 - s) * SEG, SEG)
        return [pltpu.make_async_remote_copy(
            ship.at[pl.ds(pl.multiple_of((k * 3 + a) * rows + at, SEG), SEG)], moved_cols.at[k * 3 + a, pl.ds(at, SEG)],
            col_send.at[k * 3 + a, s], col_recv.at[k * 3 + a, s], device_id=(me_row, me_col + 1), device_id_type=MESH)
            for a in range(3)]

    def row_copies(s):
        at = pl.multiple_of((windows - 1 - s) * SEG, SEG)
        to = pl.multiple_of(span - SEG - s * SEG, SEG)
        return [pltpu.make_async_remote_copy(
            fin.at[a, pl.ds(at, SEG), :], moved_rows.at[a, pl.ds(to, SEG), :],
            row_send.at[a, s], row_recv.at[a, s], device_id=(me_row + 1, me_col), device_id_type=MESH)
            for a in range(3)]

    def outer(s):
        return jnp.logical_or(s == 0, s > EARLY)

    @pl.loop(0, windows)
    def _(s):
        for kind, index in (("bottom", 0), ("top", windows - 1)):
            @pl.when(s == index)
            def _():
                for copy in loads(index, kind):
                    copy.wait()

        @pl.when(jnp.logical_and(s > EARLY, s < windows - 1))
        def _():
            for copy in loads(s, "middle"):
                copy.wait()

        window(s, list(range(n)), (d, f, c), (zr, zc), factors, tuple(range(n - 1)), store_main, GROUP, LAST)
        for k, holds in ((0, outer(s)), (1, True)):
            @pl.when(jnp.logical_and(jnp.logical_and(gives_right, s < windows - HELD), holds))
            def _():
                for copy in col_copies(s, k):
                    copy.start()

        @pl.when(jnp.logical_and(gives_down, s < span // SEG))
        def _():
            for copy in row_copies(s):
                copy.start()

        for copy in out_copies(s):
            copy.start()

    for copy in to_scalar:
        copy.wait()

    @pl.loop(0, picked.shape[0] // 16)
    def _(k):
        base = pl.multiple_of(k * 16, 16)
        rows16 = [d[pl.ds(spot_s[base + j], 1), :] for j in range(16)]
        for j in range(16):
            picked[pl.ds(base + j, 1), :] = rows16[j]

    acc[...] = jnp.zeros_like(acc)
    deep = lax.broadcasted_iota(jnp.int32, (LANES, LANES), 0)
    wide = lax.broadcasted_iota(jnp.int32, (devices, LANES), 0)

    @pl.loop(0, picked.shape[0] // LANES // LINES)
    def _(k):
        total = acc[...]
        for j in range(LINES):
            line = pl.ds(k * LINES + j, 1)
            chunk = picked[pl.ds(pl.multiple_of((k * LINES + j) * LANES, LANES), LANES), :].T
            chosen = jnp.sum(jnp.where(deep == cell_v[line, :] % LANES, chunk, 0.0), axis=0, keepdims=True)
            captured = coef_v[line, :] * jnp.maximum(chosen, 0.0)
            node = node_v[line, :]
            mine = wide == node // NODE_DEV
            pieces = []
            for _ in range(3):
                piece = captured.astype(jnp.bfloat16).astype(jnp.float32)
                pieces.append(jnp.where(mine, piece, 0.0).astype(jnp.bfloat16))
                captured = captured - piece
            within = (deep == node % NODE_DEV).astype(jnp.bfloat16)
            total = total + lax.dot_general(jnp.concatenate(pieces, axis=0), within, (((1,), (1,)), ((), ())),
                                            preferred_element_type=jnp.float32)
        acc[...] = total

    for k in range(devices):
        parts[k] = acc[pl.ds(k, 1), :] + acc[pl.ds(devices + k, 1), :] + acc[pl.ds(2 * devices + k, 1), :]

    def send(k):
        other, device = place(k)
        return pltpu.make_async_remote_copy(parts.at[other], slots.at[k], node_send.at[k], node_recv.at[k],
                                            device_id=device, device_id_type=MESH)

    @pl.loop(1, devices)
    def _(k):
        send(k).start()

    for s in range(windows - HELD, windows):
        @pl.when(gives_right)
        def _():
            for copy in col_copies(s, 0) + col_copies(s, 1):
                copy.start()

    @pl.loop(1, devices)
    def _(k):
        send(k).wait()

    note[pl.ds(0, 1), :] = parts[me] + jnp.sum(slots[pl.ds(1, devices - 1)], axis=0)
    note[pl.ds(1, 1), :] = got_top[pl.ds(2 * SUB + EDGE, 1), pl.ds(0, LANES)]
    note[pl.ds(2, 1), :] = got_left[pl.ds(2 * SUB + EDGE, 1), pl.ds(LANES, LANES)]
    note[pl.ds(3, 5), :] = jnp.zeros((5, LANES), jnp.float32)
    last = pltpu.make_async_copy(note, extra, small_sem.at[5])
    last.start()

    @pl.loop(0, windows)
    def _(s):
        for copy in out_copies(s):
            copy.wait()
        for some, holds in ((col_copies(s, 0), outer(s)), (col_copies(s, 1), True),
                            (early_copies(s), jnp.logical_not(outer(s)))):
            for copy in some:
                pl.when(jnp.logical_and(gives_right, holds))(copy.wait_send)
                pl.when(jnp.logical_and(takes_left, holds))(copy.wait_recv)
        for copy in row_copies(s):
            pl.when(jnp.logical_and(gives_down, s < span // SEG))(copy.wait_send)
            pl.when(jnp.logical_and(takes_up, s < span // SEG))(copy.wait_recv)

    last.wait()


def fused(arrays, flags, cells, nodes, coefs):
    rows, width = arrays[0].shape
    counts = (lax.axis_size("row"), lax.axis_size("col"))
    devices = counts[0] * counts[1]
    span = MAX_BLOCKS * BLOCK
    n, windows, win = width // LANES + 1, rows // SEG, SEG + 24
    tall = windows * win
    lines = cells.shape[0]
    hbm, free = pl.BlockSpec(memory_space=pltpu.HBM), pl.BlockSpec(memory_space=pl.ANY)
    vmem = lambda *shape: pltpu.VMEM(shape, jnp.float32)
    sems = lambda *shape: pltpu.SemaphoreType.DMA(shape)
    across, along = (3 * SUB, width), (3 * SUB, rows + 2 * LANES)
    raw, part = (4 * SUB, width), (3 * win, LANES)
    shapes = [(rows, width)] * 3 + [(3, span, width), (3 * MAX_BLOCKS, rows, LANES), (SUB, LANES)]
    state = vmem(n * tall, LANES)
    return pl.pallas_call(
        functools.partial(fused_kernel, counts),
        out_shape=[jax.ShapeDtypeStruct(shape, jnp.float32) for shape in shapes],
        in_specs=[hbm] * 4 + [free] + [hbm] * 3,
        out_specs=[free] * len(shapes),
        scratch_shapes=[
            state, state, state, state, vmem(tall, LANES), vmem(tall, LANES), vmem(n * win, LANES), vmem(n * win, LANES),
            vmem(3, rows, width), vmem(*part), vmem(*part), vmem(*part), vmem(*part), vmem(*part),
            vmem(EARLY, 3, SEG, LANES), vmem(3 * MAX_BLOCKS * rows, LANES), vmem(3 * SUB, rows),
            vmem(3 * SUB, rows), vmem(*raw), vmem(*raw), vmem(*across), vmem(*across), vmem(*across), vmem(*across),
            vmem(*along), vmem(*along), vmem(rows + 2 * LANES, LANES), vmem(SUB, LANES),
            pltpu.VMEM((lines, LANES), jnp.int32), pltpu.VMEM((lines, LANES), jnp.int32), vmem(lines, LANES),
            pltpu.VMEM((lines, LANES), jnp.int32), vmem(lines * LANES, LANES), vmem(3 * devices, LANES),
            vmem(devices, 1, LANES), vmem(devices, 1, LANES), vmem(SUB, LANES), pltpu.SMEM((lines * LANES,), jnp.int32),
            sems(windows, 4, n), sems(4, 4), sems(8), sems(8), sems(8), sems(3, windows), sems(6, windows),
            sems(6, windows), sems(3, windows), sems(3, windows), sems(3, windows), sems(3, windows), sems(devices),
            sems(devices), sems(lines),
        ],
        compiler_params=pltpu.CompilerParams(collective_id=0, has_side_effects=True, vmem_limit_bytes=38 << 20),
        name="fused",
    )(*arrays, flags, *[pltpu.with_memory_space_constraint(x, pltpu.HBM) for x in (cells, nodes, coefs)])


def finish_kernel(d, f, c, rows_in, cols_in, extra, out_d, out_f, out_c, out_rows, out_cols, out_node,
                  zero_rows, zero_cols, note, sem, row_sem, col_sem, note_sem):
    fetch = pltpu.make_async_copy(extra, note, note_sem.at[0])
    fetch.start()
    share = d.shape[0] // SHARES
    copies = [pltpu.make_async_copy(src.at[pl.ds(k * share, share), :], dst.at[pl.ds(k * share, share), :], sem.at[a, k])
              for a, (src, dst) in enumerate(((d, out_d), (f, out_f), (c, out_c))) for k in range(SHARES)]
    for copy in copies:
        copy.start()
    zero_rows[...] = jnp.zeros_like(zero_rows)
    zero_cols[...] = jnp.zeros_like(zero_cols)
    fetch.wait()
    given_rows = jnp.max(note[pl.ds(1, 1), :])
    given_cols = jnp.max(note[pl.ds(2, 1), :])

    def hand_on(src, hole, dst, one, keep):
        copy = pltpu.make_async_copy(src, dst, one)
        fill = pltpu.make_async_copy(hole, dst, one)
        pl.when(keep)(copy.start)
        pl.when(jnp.logical_not(keep))(fill.start)
        copies.append(copy)

    for k in range(MAX_BLOCKS):
        part = pl.ds(k * BLOCK, BLOCK)
        for a in range(3):
            hand_on(rows_in.at[a, part, :], zero_rows, out_rows.at[a, part, :], row_sem.at[a, k],
                    given_rows >= MAX_BLOCKS - k)
            hand_on(cols_in.at[k * 3 + a], zero_cols, out_cols.at[a, :, part], col_sem.at[a, k],
                    given_cols >= MAX_BLOCKS - k)
    out_node[...] = note[pl.ds(0, 1), pl.ds(0, NODE_DEV)]
    for copy in copies:
        copy.wait()


def finish(d, f, c, moved_rows, moved_cols, extra):
    rows, width = d.shape
    free, hbm = pl.BlockSpec(memory_space=pl.ANY), pl.BlockSpec(memory_space=pltpu.HBM)
    shapes = [x.shape for x in (d, f, c, moved_rows)] + [(3, rows, MAX_BLOCKS * BLOCK), (1, NODE_DEV)]
    return pl.pallas_call(
        finish_kernel,
        out_shape=[jax.ShapeDtypeStruct(shape, jnp.float32) for shape in shapes],
        in_specs=[free] * 6,
        out_specs=[hbm] * 5 + [pl.BlockSpec(memory_space=pltpu.VMEM)],
        scratch_shapes=[pltpu.VMEM((BLOCK, width), jnp.float32), pltpu.VMEM((rows, BLOCK), jnp.float32),
                        pltpu.VMEM((SUB, LANES), jnp.float32), pltpu.SemaphoreType.DMA((3, SHARES)),
                        pltpu.SemaphoreType.DMA((3, MAX_BLOCKS)), pltpu.SemaphoreType.DMA((3, MAX_BLOCKS)),
                        pltpu.SemaphoreType.DMA((1,))],
        compiler_params=pltpu.CompilerParams(vmem_limit_bytes=2 << 20),
        name="finish",
    )(d, f, c, moved_rows, moved_cols, extra)


def body(
    depth,
    ground,
    flow_rows,
    flow_cols,
    wet_tiles,
    inlet_cell,
    inlet_node,
    inlet_coef,
    shift_rows,
    shift_cols,
):
    flat = lambda x: x.reshape(-1, LANES)
    flags = sum(jnp.pad(value, ((k, SUB - 1 - k), (0, LANES - 1)))
                for k, value in enumerate((wet_tiles, shift_rows, shift_cols))).astype(jnp.float32)
    results = fused((depth, ground, flow_rows, flow_cols), flags,
                    flat(inlet_cell), flat(inlet_node), flat(inlet_coef))
    depth, flow_rows, flow_cols, moved_rows, moved_cols, node_inflow = finish(*results)
    return (depth, flow_rows, flow_cols, node_inflow[0], moved_rows, moved_cols)


def solution(mesh):
    return jax.shard_map(
        body,
        mesh=mesh,
        in_specs=(
            P("row", "col"),
            P("row", "col"),
            P("row", "col"),
            P("row", "col"),
            P("row", "col"),
            P("row", "col", None),
            P("row", "col", None),
            P("row", "col", None),
            P("row", "col"),
            P("row", "col"),
        ),
        out_specs=(
            P("row", "col"),
            P("row", "col"),
            P("row", "col"),
            P(("row", "col")),
            P(None, "row", "col"),
            P(None, "row", "col"),
        ),
        check_vma=False,
    )
```
